128 devices in a mesh: px: 8 (over z, core), py: 16 (over y, x).
Axes of the slice: x: 4, y: 4, z: 4, core: 2. Of those that a mesh axis runs over, the one named last changes fastest.
Arguments:
- velocity: float32 [3, 512, 512, 128], P(None, ('px', 'py')), may hold values from -6 to 6
- layer_depth: float32 [128], replicated, may hold values from 0.5 to 2
- vertical_modes: float32 [128, 128], replicated, may hold values from -0.5 to 0.5
- vertical_synthesis: float32 [128, 128], replicated, may hold values from -0.5 to 0.5
- mode_eigen: float32 [128], replicated, may hold values from 0.0025 to 2
- boundary_tracers: float32 [2, 512, 512], P(None, ('px', 'py')), may hold values from -6 to 6
- friction_speed: float32 [512, 512], P(('px', 'py')), may hold values from 0.3 to 3
- draft_level: int32 [512, 512], P(('px', 'py')), may hold values from 0 to 127
- tile_offset: int32 [128], replicated, may hold values from 0 to 127, as said below
- draft_count: int32 [128, 128], P(('px', 'py')), may hold values from 1 to 8, as said below
- draft_list: int32 [128, 128, 8], P(('px', 'py')), may hold values from 0 to 15, as said below
- exchange_coeff: float32 [262144], P(('px', 'py')), may hold values from 0.5 to 2
- ice_thickness: float32 [262144], P(('px', 'py')), may hold values from 1 to 3
Outputs:
- pressure: float32 [512, 512, 128], P(('px', 'py'))
- thickness_new: float32 [262144], P(('px', 'py'))
The draws below stay inside these ranges and needn't reach their ends.
Inputs may be any that keep to these rules, and one draw needn't show every extreme that they name: `tile_offset`: A permutation of 0 to 127. `draft_count`: every draw has an owner all of whose tile slots receive 8 draft cells. `draft_list`: the 8 positions of one tile's list are different.
All inputs are finite; a program needn't handle non-finite values.
Results may differ from the reference program's by a relative error of at most 0.00029.
Values sent between devices are 32-bit elements; how exact they have to be, the bound alone decides.
A program may use at most 64 MiB of HBM per device.

```python
import math
import jax
import jax.numpy as jnp
from jax import lax

NX = 512
NY = 512
NZ = 128
RANKS = 128
TILE_DEV = 128
ROWS_DEV = 4
TILE_W = 4
TILE_COLS = 16
CAP = 8


def plan_tiles(key):
    offsets = jax.random.permutation(jax.random.fold_in(key, 7), RANKS)[:TILE_DEV].astype(jnp.int32)
    owner_levels = jax.random.randint(jax.random.fold_in(key, 8), (RANKS,), 1, 5)
    full_owner = jax.random.randint(jax.random.fold_in(key, 9), (), 0, RANKS)
    owner = (jnp.arange(RANKS, dtype=jnp.int32)[:, None] + offsets[None, :]) % RANKS
    tile_level = owner_levels[owner]
    lowest = CAP * tile_level // 8
    highest = CAP * tile_level // 4
    counts = jax.random.randint(jax.random.fold_in(key, 10), (RANKS, TILE_DEV), lowest, highest + 1)
    counts = jnp.where(owner == full_owner, CAP, counts)
    return (offsets, counts.astype(jnp.int32))


def draw_tile_offset(key, part):
    return plan_tiles(key)[0]


def draw_draft_count(key, part):
    return plan_tiles(key)[1]


def draw_draft_list(key, part):
    scores = jax.random.randint(jax.random.fold_in(key, 11), (RANKS, TILE_DEV, TILE_COLS), 0, 2 ** 20)
    scores = scores * TILE_COLS + jnp.arange(TILE_COLS, dtype=jnp.int32)
    return jnp.argsort(scores, axis=-1)[:, :, :CAP].astype(jnp.int32)


def draw_mode_eigen(key, part):
    low_end = math.log(0.0025)
    high_end = math.log(2.0)
    fraction = jax.random.uniform(jax.random.fold_in(key, 21), (NZ,), jnp.float32)
    values = jnp.exp(low_end + (high_end - low_end) * fraction)
    return jnp.clip(values, 0.0025, 2.0).astype(jnp.float32)


def place_ends(array, key, low, high):
    extent = array.shape
    place = [jax.random.randint(jax.random.fold_in(key, axis), (), 0, extent[axis]) for axis in range(len(extent))]
    array = array.at[tuple(place)].set(low)
    longest = extent.index(max(extent))
    place[longest] = (place[longest] + 1) % extent[longest]
    return array.at[tuple(place)].set(high)


def block_scale(own_key, shape, shards, smallest, largest):
    level, own = 1.0, jax.random.fold_in(own_key, 6)
    for dim, shards_of in shards:
        heights = jnp.exp(jax.random.uniform(jax.random.fold_in(own, dim), (shards_of,), jnp.float32, smallest / len(shards), largest / len(shards)))
        level = level * jnp.repeat(heights, shape[dim] // shards_of).reshape([-1 if axis == dim else 1 for axis in range(len(shape))])
    return level


def scatter_about(stream_key, shape, width, most, split=(), held_as=jnp.bfloat16):
    factor_of = block_scale(stream_key, shape, split, -0.22, 0.18) if split else 1.0
    result = jax.random.normal(stream_key, shape, jnp.float32) * width * factor_of
    return jnp.minimum(jnp.maximum(result, -most), most).astype(held_as)


def setup_inputs(seed: int = 0) -> dict:
    splits = jax.random.split(jax.random.key(seed), 14)
    return {
        "velocity": scatter_about(splits[0], (3, NX, NY, NZ), 1.0, 6.0, ((1, 128),), jnp.float32),
        "layer_depth": jnp.clip(jnp.exp(jax.random.uniform(splits[1], (NZ,), jnp.float32, math.log(0.5), math.log(2.0))), 0.5, 2.0),
        "vertical_modes": scatter_about(splits[2], (NZ, NZ), NZ ** -0.5, 0.5, (), jnp.float32),
        "vertical_synthesis": scatter_about(splits[3], (NZ, NZ), NZ ** -0.5, 0.5, (), jnp.float32),
        "mode_eigen": draw_mode_eigen(jax.random.fold_in(splits[13], 71), 0),
        "boundary_tracers": scatter_about(splits[5], (2, NX, NY), 1.0, 6.0, ((1, 128),), jnp.float32),
        "friction_speed": jnp.clip(jnp.exp(math.log(3.0) - 2.3025851 * jax.random.uniform(splits[6], (NX, NY), jnp.float32) ** block_scale(splits[6], (NX, NY), ((0, 128),), -0.2, 0.2)), 0.3, 3.0),
        "draft_level": place_ends(jax.random.randint(splits[7], (NX, NY), 0, NZ), jax.random.fold_in(splits[7], 1), 0, NZ - 1).astype(jnp.int32),
        "tile_offset": draw_tile_offset(jax.random.fold_in(splits[13], 71), 0),
        "draft_count": draw_draft_count(jax.random.fold_in(splits[13], 71), 0),
        "draft_list": draw_draft_list(jax.random.fold_in(splits[13], 71), 0),
        "exchange_coeff": jnp.clip(jnp.exp(math.log(2.0) - 1.3862944 * jax.random.uniform(splits[11], (NX * NY,), jnp.float32) ** block_scale(splits[11], (NX * NY,), ((0, 128),), -0.2, 0.2)), 0.5, 2.0),
        "ice_thickness": jnp.clip(1.0 + 2.0 * jax.random.uniform(splits[12], (NX * NY,), jnp.float32) ** block_scale(splits[12], (NX * NY,), ((0, 128),), -0.2, 0.2), 1.0, 3.0),
    }


EXACT = lax.Precision.HIGHEST

def hartley_table(length, row_index, col_index):
    product = row_index[:, None] * col_index[None, :] % length
    angle = product.astype(jnp.float32) * (2.0 * math.pi / length)
    return (jnp.cos(angle) + jnp.sin(angle)) / math.sqrt(length)

def wave_number(length, index):
    angle = (index % length).astype(jnp.float32) * (2.0 * math.pi / length)
    return 2.0 - 2.0 * jnp.cos(angle)

def melt_formula(coeff, tracers):
    thermal = tracers[0] - 0.6 * tracers[1] + 1.5 * tracers[3] - 0.5
    return coeff * tracers[2] * thermal

def reference(velocity, layer_depth, vertical_modes, vertical_synthesis, mode_eigen, boundary_tracers, friction_speed, draft_level, tile_offset, draft_count, draft_list, exchange_coeff, ice_thickness):
    rank_index = jnp.arange(RANKS, dtype=jnp.int32)[:, None, None]
    tile_index = jnp.arange(TILE_DEV, dtype=jnp.int32)[None, :, None]
    live_slot = jnp.arange(CAP, dtype=jnp.int32)[None, None, :] < draft_count[:, :, None]
    row_global = rank_index * ROWS_DEV + draft_list // TILE_W
    col_global = tile_index * TILE_W + draft_list % TILE_W
    flat = row_global * NY + col_global
    owner = (rank_index + tile_offset[None, :, None]) % RANKS
    shelf_index = owner * (TILE_DEV * TILE_COLS) + tile_index * TILE_COLS + draft_list
    level_flat = draft_level.reshape(NX * NY)
    level_frac = (level_flat[flat].astype(jnp.float32) + 0.5) / NZ
    tracer_flat = boundary_tracers.reshape(2, NX * NY)
    rows = jnp.stack([tracer_flat[0][flat], tracer_flat[1][flat], friction_speed.reshape(NX * NY)[flat], level_frac])
    melt_rate = melt_formula(exchange_coeff[shelf_index], rows)
    thinning = jnp.zeros((NX * NY,), jnp.float32).at[shelf_index].add(jnp.where(live_slot, 0.3 * melt_rate, 0.0))
    thickness_new = ice_thickness - thinning
    melt_column = jnp.zeros((NX * NY,), jnp.float32).at[flat].add(jnp.where(live_slot, melt_rate, 0.0))
    source_rate = melt_column / layer_depth[level_flat]
    level_range = jnp.arange(NZ, dtype=jnp.int32)
    source_field = jnp.where(level_flat[:, None] == level_range[None, :], source_rate[:, None], 0.0).reshape(NX, NY, NZ)
    east_flow = velocity[0]
    north_flow = velocity[1]
    up_flow = velocity[2]
    east_diff = east_flow - jnp.roll(east_flow, 1, axis=0)
    north_diff = north_flow - jnp.roll(north_flow, 1, axis=1)
    below = jnp.concatenate([jnp.zeros_like(up_flow[:, :, :1]), up_flow[:, :, :NZ - 1]], axis=2)
    up_diff = (up_flow - below) / layer_depth
    forcing = east_diff + north_diff + up_diff + source_field
    modal_field = jnp.dot(forcing.reshape(NX * NY, NZ), vertical_modes, precision=EXACT).reshape(NX, NY, NZ)
    range_x = jnp.arange(NX, dtype=jnp.int32)
    range_y = jnp.arange(NY, dtype=jnp.int32)
    table_x = hartley_table(NX, range_x, range_x)
    table_y = hartley_table(NY, range_y, range_y)
    along_y = jnp.einsum('jy,xyk->xjk', table_y, modal_field, precision=EXACT)
    along_x = jnp.einsum('ix,xjk->ijk', table_x, along_y, precision=EXACT)
    denom = wave_number(NX, range_x)[:, None, None] + wave_number(NY, range_y)[None, :, None] + mode_eigen[None, None, :]
    solved = along_x / denom
    back_x = jnp.einsum('il,ljk->ijk', table_x, solved, precision=EXACT)
    back_y = jnp.einsum('ym,xmk->xyk', table_y, back_x, precision=EXACT)
    pressure = jnp.dot(back_y.reshape(NX * NY, NZ), vertical_synthesis, precision=EXACT).reshape(NX, NY, NZ)
    return (pressure, thickness_new)
```

```python
import functools
import math

import jax
import jax.numpy as jnp
import numpy as np
from jax import lax
from jax.experimental import pallas as pl
from jax.experimental.pallas import tpu as pltpu
from jax.sharding import PartitionSpec as P

NX = 512
NY = 512
NZ = 128
RANKS = 128
ROWS = 4
NB = 4
BLK = NY // NB
PER_BLK = RANKS // NB
MESH = pl.DeviceIdType.MESH
F32 = jnp.float32
BF16 = jnp.bfloat16


def hartley(length):
    index = np.arange(length)
    angle = (np.outer(index, index) % length) * (2.0 * math.pi / length)
    return (np.cos(angle) + np.sin(angle)) / math.sqrt(length)


def split_table(table):
    whole = jnp.asarray(table, F32)
    high = np.asarray(table, np.float32).astype(jnp.bfloat16)
    low = (np.asarray(table, np.float32) - high.astype(np.float32)).astype(jnp.bfloat16)
    del whole
    return high, low


def eigen(length):
    return 2.0 - 2.0 * np.cos(2.0 * math.pi * np.arange(length) / length)


def split(x):
    high = x.astype(BF16)
    return high, (x - high.astype(F32)).astype(BF16)


def mm(a, b):
    return jnp.dot(a, b, preferred_element_type=F32)


def mm_exact_left(a, x):
    high, low = split(x)
    return mm(a, high) + mm(a, low)


def mm_exact_right(x, b):
    high, low = split(x)
    return mm(high, b) + mm(low, b)


def mm3(x, b_high, b_low):
    high, low = split(x)
    return mm(high, b_high) + mm(low, b_high) + mm(high, b_low)


def iota(shape, axis):
    return lax.broadcasted_iota(jnp.int32, shape, axis)


def kernel(
    vel_hbm,
    hh_hbm,
    hl_hbm,
    hxf_ref,
    hxi_ref,
    lam_ref,
    lamx_ref,
    depth_ref,
    modes_ref,
    synth_ref,
    eig_ref,
    trac_ref,
    fric_ref,
    lvl_ref,
    off_ref,
    cnt_ref,
    list_ref,
    coeff_ref,
    ice_ref,
    out_hbm,
    thick_ref,
    vel,
    h3,
    x3,
    modal,
    spec,
    wrow,
    outv,
    cs,
    cr,
    ms,
    mr,
    s2,
    r2,
    s3,
    r3,
    load_sem,
    out_sem,
    c_send,
    c_recv,
    m_send,
    m_recv,
    f_send,
    f_recv,
    b_send,
    b_recv,
):
    px = lax.axis_index("px")
    py = lax.axis_index("py")
    my_z, my_c, my_y, my_x = px // 2, px % 2, py // 4, py % 4
    me = px * 16 + py
    my_class = (my_x + my_y + my_z) % NB
    my_slot = my_class * 32 + my_c * 16 + my_y * 4 + my_x

    loads = [pltpu.make_async_copy(vel_hbm, vel, load_sem.at[0])]
    for part, table in enumerate((hh_hbm, hh_hbm, hl_hbm)):
        loads.append(
            pltpu.make_async_copy(
                table, h3.at[:, pl.ds(part * NY, NY)], load_sem.at[1 + part]
            )
        )
    for load in loads:
        load.start()

    def partner(step):
        mixed = (step * 37) % RANKS
        dz, dy, dx, dc = mixed % 4, (mixed // 4) % 4, (mixed // 16) % 4, mixed // 64
        pz, pc = (my_z + dz) % 4, (my_c + dc) % 2
        qy, qx = (my_y + dy) % 4, (my_x + dx) % 4
        return pz * 2 + pc, qy * 4 + qx

    barrier = pltpu.get_barrier_semaphore()

    def greet(step, carry):
        pl.semaphore_signal(barrier, inc=1, device_id=partner(step), device_id_type=MESH)
        return carry

    lax.fori_loop(1, RANKS, greet, 0)

    off = off_ref[...]
    sub = iota((RANKS, RANKS), 0)
    lane = iota((RANKS, RANKS), 1)
    from_owner = ((me - off + RANKS) % RANKS == sub).astype(BF16)
    tile_row = (iota((RANKS, 16), 0) // 8 == iota((RANKS, 16), 1)).astype(BF16)
    pick = mm(from_owner, tile_row)
    send_c = jnp.dot(pick, coeff_ref[...], precision=lax.Precision.HIGHEST)
    cs[pl.ds(0, RANKS, stride=8), :] = send_c
    cr[pl.ds(pl.multiple_of(me * 8, 8), 1), :] = cs[pl.ds(pl.multiple_of(me * 8, 8), 1), :]

    pl.semaphore_wait(barrier, RANKS - 1)

    def send_small(src, dst, send_sem, recv_sem):
        def step_of(step, carry):
            qx, qy = partner(step)
            rank = qx * 16 + qy
            pltpu.make_async_remote_copy(
                src_ref=src.at[pl.ds(pl.multiple_of(rank * 8, 8), 1), :],
                dst_ref=dst.at[pl.ds(pl.multiple_of(me * 8, 8), 1), :],
                send_sem=send_sem,
                recv_sem=recv_sem,
                device_id=(qx, qy),
                device_id_type=MESH,
            ).start()
            return carry

        lax.fori_loop(1, RANKS, step_of, 0)

    def wait_rows(ref, rows, sem):
        pltpu.make_async_copy(ref.at[pl.ds(0, rows), :], ref.at[pl.ds(0, rows), :], sem).wait()

    send_small(cs, cr, c_send, c_recv)

    depth = depth_ref[...]
    inv_depth = 1.0 / depth
    diag = sub == lane
    inv_depth_col = jnp.sum(jnp.where(diag, inv_depth, 0.0), axis=1, keepdims=True)
    level = lvl_ref[...].astype(F32)
    thermal = trac_ref[0] - 0.6 * trac_ref[1] + 1.5 * ((level + 0.5) / NZ) - 0.5
    factor = fric_ref[...] * thermal
    rows_lane = (iota((ROWS, NZ), 1) % 16 // 4 == iota((ROWS, NZ), 0)).astype(F32)
    contract_first = (((0,), (0,)), ((), ()))
    factor_lanes = lax.dot_general(
        factor, rows_lane, contract_first, precision=lax.Precision.HIGHEST,
        preferred_element_type=F32,
    )
    y_sub = iota((NY, NZ), 0)
    y_lane = iota((NY, NZ), 1)
    in_tile = y_sub % 32 == 4 * (y_lane // 16) + y_lane % 4
    tile_of_y = (iota((NY, RANKS), 0) // 4 == iota((NY, RANKS), 1)).astype(BF16)
    tile_from_y = (iota((RANKS, NY), 1) // 4 == iota((RANKS, NY), 0)).astype(BF16)
    by_tile = mm_exact_left(tile_from_y, jnp.where(in_tile, factor_lanes, 0.0))
    count = jnp.sum(jnp.where(diag, cnt_ref[...].astype(F32), 0.0), axis=1, keepdims=True)
    cells = list_ref[...].reshape(RANKS, 8)
    cells = jnp.where(iota((RANKS, 8), 1).astype(F32) < count, cells, -1)
    live = cells[:, 0:1] == lane % 16
    for slot in range(1, 8):
        live = jnp.logical_or(live, cells[:, slot : slot + 1] == lane % 16)
    to_owner = ((me + off) % RANKS == sub).astype(BF16)
    factor_owner = mm_exact_left(to_owner, jnp.where(live, by_tile, 0.0))
    owner_of_y = lax.dot_general(
        tile_of_y, to_owner, (((1,), (1,)), ((), ())), preferred_element_type=F32
    ).astype(BF16)

    modes = modes_ref[...]
    mode_high, mode_low = split(modes)
    scaled_high, scaled_low = split(modes * inv_depth_col)
    spread = (iota((ROWS, ROWS * NZ), 1) // NZ == iota((ROWS, ROWS * NZ), 0)).astype(F32)
    level_lanes = lax.dot_general(
        level, spread, contract_first, preferred_element_type=F32
    )
    for r in range(ROWS):
        hot = (level_lanes[:, r * NZ : (r + 1) * NZ] == y_lane.astype(F32)).astype(BF16)
        wrow[:, r * NZ : (r + 1) * NZ] = mm(hot, scaled_high) + mm(hot, scaled_low)

    loads[0].wait()
    for r in range(ROWS + 1):
        if r < ROWS:
            east, north, up = vel[0, r], vel[1, r], vel[2, r]
            if r > 0:
                east = east - vel[0, r - 1]
            below = jnp.where(y_lane == 0, 0.0, pltpu.roll(up, 1, axis=1))
            flow = east + (north - pltpu.roll(north, 1, axis=0)) + (up - below) * inv_depth
        else:
            flow = vel[0, ROWS - 1]
        field = mm3(flow, mode_high, mode_low)
        if r < ROWS:
            modal[:, r * NZ : (r + 1) * NZ] = field
        else:
            high, low = split(field)
            x3[0:NY, r * NZ : (r + 1) * NZ] = high
            x3[NY : 2 * NY, r * NZ : (r + 1) * NZ] = low
            x3[2 * NY : 3 * NY, r * NZ : (r + 1) * NZ] = high
    spread_rows = (
        iota((NZ, ROWS * NZ), 0) % 16 // 4 == iota((NZ, ROWS * NZ), 1) // NZ
    ).astype(BF16)

    wait_rows(cr, RANKS - 1, c_recv)
    melt = cr[pl.ds(0, RANKS, stride=8), :] * factor_owner
    ms[pl.ds(0, RANKS, stride=8), :] = melt
    by_y = jnp.where(in_tile, mm_exact_left(owner_of_y, melt), 0.0)
    melt_lanes = mm_exact_right(by_y, spread_rows)
    high, low = split(modal[...] + melt_lanes * wrow[...])
    x3[0:NY, 0 : ROWS * NZ] = high
    x3[NY : 2 * NY, 0 : ROWS * NZ] = low
    x3[2 * NY : 3 * NY, 0 : ROWS * NZ] = high
    for load in loads[1:]:
        load.wait()

    eig = eig_ref[...]

    def block_step(step, carry):
        block = (my_class + step) % NB
        start = pl.multiple_of(block * BLK, BLK)
        rows = pl.ds(start, BLK)
        part = mm(h3[rows, :], x3[...])
        spec[rows, :] = part
        t = 2.0 + (lam_ref[rows, :] + eig)
        u2 = t * t - 1.0
        u3 = t * (t * t - 2.0)
        f = [part[:, r * NZ : (r + 1) * NZ] for r in range(ROWS + 1)]
        s2[pl.ds(2 * start, BLK, stride=2), :] = u3 * f[0] + u2 * f[1] + t * f[2] + f[3]
        s2[pl.ds(2 * start + 1, BLK, stride=2), :] = f[1] + t * f[2] + u2 * f[3] - u3 * f[4]

        def send(index, inner):
            c, y, x = index // 16, (index // 4) % 4, index % 4
            c, y, x = (c + my_c) % 2, (y + my_y) % 4, (x + my_x) % 4
            z = (block - x - y + 8) % 4
            slot = block * PER_BLK + c * 16 + y * 4 + x

            @pl.when(slot != my_slot)
            def _():
                pltpu.make_async_remote_copy(
                    src_ref=s2.at[pl.ds(pl.multiple_of(slot * 8, 8), 8), :],
                    dst_ref=r2.at[pl.ds(pl.multiple_of(me * 8, 8), 8), :],
                    send_sem=f_send,
                    recv_sem=f_recv,
                    device_id=(z * 2 + c, y * 4 + x),
                    device_id_type=MESH,
                ).start()

            return inner

        lax.fori_loop(0, PER_BLK, send, 0)
        return carry

    lax.fori_loop(0, NB, block_step, 0)
    r2[pl.ds(pl.multiple_of(me * 8, 8), 8), :] = s2[pl.ds(pl.multiple_of(my_slot * 8, 8), 8), :]

    send_small(ms, mr, m_send, m_recv)
    mr[pl.ds(pl.multiple_of(me * 8, 8), 1), :] = ms[pl.ds(pl.multiple_of(me * 8, 8), 1), :]

    t = 2.0 + (lam_ref[...] + eig)
    u2 = t * t - 1.0
    u3 = t * (t * t - 2.0)
    w3 = 1.0 / u3
    w1 = u2 * w3
    w2 = t * w3
    f1, f2, f3 = (spec[:, r * NZ : (r + 1) * NZ] for r in range(1, ROWS))
    modal[:, 0:NZ] = w1 * f1 + w2 * f2 + w3 * f3
    modal[:, NZ : 2 * NZ] = w2 * (f1 + t * f2 + f3)
    modal[:, 2 * NZ : 3 * NZ] = w3 * f1 + w2 * f2 + w1 * f3
    wrow[:, 0:NZ] = w1
    wrow[:, NZ : 2 * NZ] = w2
    wrow[:, 2 * NZ : 3 * NZ] = w3

    inverse = []
    for jj in range(4):
        shift = lam_ref[pl.ds(my_slot * 4 + jj, 1), :] + eig
        edge = 2.0 + shift
        inverse.append(1.0 / (edge * edge * shift * (4.0 + shift) + lamx_ref[...]))
    wait_rows(r2, (RANKS - 1) * 8, f_recv)
    for jj in range(4):
        first = r2[pl.ds(2 * jj, RANKS, stride=8), :]
        second = r2[pl.ds(2 * jj + 1, RANKS, stride=8), :]
        first_high, first_low = split(first)
        second_high, second_low = split(second)
        stacked = jnp.concatenate(
            [first_high, second_high, first_low, second_low, first_high, second_high], axis=0
        )
        solved = mm(hxf_ref[...], stacked) * inverse[jj]
        high, low = split(solved)
        both = mm(hxi_ref[...], jnp.concatenate([high, low, high], axis=0))
        s3[pl.ds(2 * jj, RANKS, stride=8), :] = both[0:RANKS]
        s3[pl.ds(2 * jj + 1, RANKS, stride=8), :] = both[RANKS : 2 * RANKS]

    def send_back(step, carry):
        qx, qy = partner(step)
        rank = qx * 16 + qy
        pltpu.make_async_remote_copy(
            src_ref=s3.at[pl.ds(pl.multiple_of(rank * 8, 8), 8), :],
            dst_ref=r3.at[pl.ds(pl.multiple_of(my_slot * 8, 8), 8), :],
            send_sem=b_send,
            recv_sem=b_recv,
            device_id=(qx, qy),
            device_id_type=MESH,
        ).start()
        return carry

    lax.fori_loop(1, RANKS, send_back, 0)
    r3[pl.ds(pl.multiple_of(my_slot * 8, 8), 8), :] = s3[pl.ds(pl.multiple_of(me * 8, 8), 8), :]

    wait_rows(mr, RANKS - 1, m_recv)
    thinning = lax.dot_general(
        pick, mr[pl.ds(0, RANKS, stride=8), :], contract_first,
        precision=lax.Precision.HIGHEST, preferred_element_type=F32,
    )
    thick_ref[...] = ice_ref[...] - 0.3 * thinning
    synth_high, synth_low = split(synth_ref[...])

    wait_rows(r3, (RANKS - 1) * 8, b_recv)
    q0 = r3[pl.ds(0, NY, stride=2), :]
    q1 = r3[pl.ds(1, NY, stride=2), :]
    w1, w2, w3 = (wrow[:, r * NZ : (r + 1) * NZ] for r in range(3))
    fields = [
        q0,
        w1 * q0 + w3 * q1 + modal[:, 0:NZ],
        w2 * (q0 + q1) + modal[:, NZ : 2 * NZ],
        w3 * q0 + w1 * q1 + modal[:, 2 * NZ : 3 * NZ],
    ]
    for r in range(ROWS):
        high, low = split(fields[r])
        x3[0:NY, r * NZ : (r + 1) * NZ] = high
        x3[NY : 2 * NY, r * NZ : (r + 1) * NZ] = low
        x3[2 * NY : 3 * NY, r * NZ : (r + 1) * NZ] = high

    def out_step(block, carry):
        rows = pl.ds(pl.multiple_of(block * BLK, BLK), BLK)
        part = mm(h3[rows, :], x3[:, 0 : ROWS * NZ])
        for r in range(ROWS):
            outv[r, rows, :] = mm3(part[:, r * NZ : (r + 1) * NZ], synth_high, synth_low)
        return carry

    lax.fori_loop(0, NB, out_step, 0)
    store = pltpu.make_async_copy(outv, out_hbm, out_sem)
    store.start()
    wait_rows(cs, RANKS - 1, c_send)
    wait_rows(ms, RANKS - 1, m_send)
    wait_rows(s2, (RANKS - 1) * 8, f_send)
    wait_rows(s3, (RANKS - 1) * 8, b_send)
    store.wait()


def body(
    velocity,
    layer_depth,
    vertical_modes,
    vertical_synthesis,
    mode_eigen,
    boundary_tracers,
    friction_speed,
    draft_level,
    tile_offset,
    draft_count,
    draft_list,
    exchange_coeff,
    ice_thickness,
):
    hh, hl = split_table(hartley(NY))
    small = hartley(RANKS)
    following = (np.arange(RANKS) + 1) % RANKS
    fwd_high, fwd_low = split_table(np.concatenate([small, small[:, following]], axis=1))
    inv_high, inv_low = split_table(np.concatenate([small, small[following]], axis=0))
    hxf = np.concatenate([fwd_high, fwd_high, fwd_low], axis=1)
    hxi = np.concatenate([inv_high, inv_high, inv_low], axis=1)
    lam = np.repeat(eigen(NY)[:, None], NZ, axis=1).astype(np.float32)
    lamx = np.repeat(eigen(RANKS)[:, None], NZ, axis=1).astype(np.float32)
    vmem = pl.BlockSpec(memory_space=pltpu.VMEM)
    hbm = pl.BlockSpec(memory_space=pl.ANY)
    tiles = (RANKS * 8, NZ)
    pressure, thickness = pl.pallas_call(
        kernel,
        out_shape=(
            jax.ShapeDtypeStruct((ROWS, NY, NZ), F32),
            jax.ShapeDtypeStruct((16, 128), F32),
        ),
        in_specs=[hbm] * 3 + [vmem] * 16,
        out_specs=(hbm, vmem),
        scratch_shapes=[
            pltpu.VMEM((3, ROWS, NY, NZ), F32),
            pltpu.VMEM((NY, 3 * NY), BF16),
            pltpu.VMEM((3 * NY, (ROWS + 1) * NZ), BF16),
            pltpu.VMEM((NY, ROWS * NZ), F32),
            pltpu.VMEM((NY, (ROWS + 1) * NZ), F32),
            pltpu.VMEM((NY, ROWS * NZ), F32),
            pltpu.VMEM((ROWS, NY, NZ), F32),
        ]
        + [pltpu.VMEM(tiles, F32)] * 8
        + [pltpu.SemaphoreType.DMA((4,))]
        + [pltpu.SemaphoreType.DMA] * 9,
        compiler_params=pltpu.CompilerParams(
            collective_id=0, has_side_effects=True, vmem_limit_bytes=56 * 2**20
        ),
    )(
        velocity,
        hh,
        hl,
        hxf,
        hxi,
        lam,
        lamx,
        layer_depth.reshape(1, NZ),
        vertical_modes,
        vertical_synthesis,
        mode_eigen.reshape(1, NZ),
        boundary_tracers,
        friction_speed,
        draft_level,
        tile_offset.reshape(1, RANKS),
        draft_count,
        draft_list,
        exchange_coeff.reshape(16, 128),
        ice_thickness.reshape(16, 128),
    )
    return (pressure, thickness.reshape(2048))


def solution(mesh):
    in_specs = (
        P(None, ("px", "py"), None, None),
        P(),
        P(),
        P(),
        P(),
        P(None, ("px", "py"), None),
        P(("px", "py"), None),
        P(("px", "py"), None),
        P(),
        P(("px", "py"), None),
        P(("px", "py"), None, None),
        P(("px", "py")),
        P(("px", "py")),
    )
    out_specs = (P(("px", "py"), None, None), P(("px", "py")))
    return jax.shard_map(body, mesh=mesh, in_specs=in_specs, out_specs=out_specs, check_vma=False)
```

```python
import math

import jax
import jax.numpy as jnp
import numpy as np
from jax import lax
from jax.experimental import pallas as pl
from jax.experimental.pallas import tpu as pltpu
from jax.sharding import PartitionSpec as P

NX = 512
NY = 512
NZ = 128
RANKS = 128
ROWS = 4
NB = 4
BLK = NY // NB
MESH = pl.DeviceIdType.MESH
F32 = jnp.float32
BF16 = jnp.bfloat16


def hartley(length):
    index = np.arange(length)
    angle = (np.outer(index, index) % length) * (2.0 * math.pi / length)
    return (np.cos(angle) + np.sin(angle)) / math.sqrt(length)


def split_table(table):
    high = np.asarray(table, np.float32).astype(jnp.bfloat16)
    low = (np.asarray(table, np.float32) - high.astype(np.float32)).astype(jnp.bfloat16)
    return high, low


def eigen(length):
    return 2.0 - 2.0 * np.cos(2.0 * math.pi * np.arange(length) / length)


def split(x):
    high = x.astype(BF16)
    return high, (x - high.astype(F32)).astype(BF16)


def mm(a, b):
    return jnp.dot(a, b, preferred_element_type=F32)


def mm_exact_left(a, x):
    high, low = split(x)
    return mm(a, high) + mm(a, low)


def mm_exact_right(x, b):
    high, low = split(x)
    return mm(high, b) + mm(low, b)


def mm3(x, b_high, b_low):
    high, low = split(x)
    return mm(high, b_high) + mm(low, b_high) + mm(high, b_low)


def iota(shape, axis):
    return lax.broadcasted_iota(jnp.int32, shape, axis)


def kernel(
    vel_hbm,
    hh_hbm,
    hl_hbm,
    hxf_ref,
    hxi_ref,
    lam_ref,
    lamx_ref,
    depth_ref,
    modes_ref,
    synth_ref,
    eig_ref,
    trac_ref,
    fric_ref,
    lvl_ref,
    off_ref,
    cnt_ref,
    list_ref,
    coeff_ref,
    ice_ref,
    out_hbm,
    thick_ref,
    vel,
    h3,
    x3,
    modal,
    spec,
    wrow,
    outv,
    xk,
    inv,
    xs,
    xr,
    yr,
    ps,
    pr,
    s2,
    r2,
    s3,
    r3,
    load_sem,
    out_sem,
    near_send,
    near_recv,
    f_send,
    f_recv,
    b_send,
    b_recv,
):
    px = lax.axis_index("px")
    py = lax.axis_index("py")
    my_z, my_c, my_y, my_x = px // 2, px % 2, py // 4, py % 4
    me = px * 16 + py

    loads = [pltpu.make_async_copy(vel_hbm, vel, load_sem.at[0])]
    for part, table in enumerate((hh_hbm, hh_hbm, hl_hbm)):
        loads.append(
            pltpu.make_async_copy(
                table, h3.at[:, pl.ds(part * NY, NY)], load_sem.at[1 + part]
            )
        )
    for load in loads:
        load.start()

    x_of = [(my_x + d) % 4 for d in range(4)]
    y_of = [(my_y + d) % 4 for d in range(4)]
    p_of = [(px + d) % 8 for d in range(8)]
    x_peers = [(px, my_y * 4 + x_of[d]) for d in range(1, 4)]
    y_peers = [(px, y_of[d] * 4 + my_x) for d in range(1, 4)]
    p_peers = [(p_of[d], py) for d in range(1, 8)]
    barrier = pltpu.get_barrier_semaphore()
    peers = x_peers + y_peers + p_peers
    for peer in peers:
        pl.semaphore_signal(barrier, inc=1, device_id=peer, device_id_type=MESH)

    off = off_ref[...]
    sub = iota((RANKS, RANKS), 0)
    lane = iota((RANKS, RANKS), 1)
    rank_of_sub = sub % 8 * 16 + sub // 8 % 4 * 4 + sub // 32
    tile_row = (iota((RANKS, 16), 0) // 8 == iota((RANKS, 16), 1)).astype(BF16)
    give = (me - off + RANKS) % RANKS
    pick_send = mm((give == rank_of_sub).astype(BF16), tile_row)
    send_c = jnp.dot(pick_send, coeff_ref[...], precision=lax.Precision.HIGHEST)
    xs[...] = send_c.reshape(4, 4, 8, NZ)
    xr[my_x] = xs[my_x]

    def copies_near(stage, sources, targets, devices):
        return [
            pltpu.make_async_remote_copy(
                src_ref=source,
                dst_ref=target,
                send_sem=near_send.at[stage],
                recv_sem=near_recv.at[stage],
                device_id=device,
                device_id_type=MESH,
            )
            for source, target, device in zip(sources, targets, devices)
        ]

    pl.semaphore_wait(barrier, len(peers))
    for copy in copies_near(0, [xs.at[x] for x in x_of[1:]], [xr.at[my_x]] * 3, x_peers):
        copy.start()

    inv_depth = 1.0 / depth_ref[...]
    inv_depth_col = jnp.sum(jnp.where(sub == lane, inv_depth, 0.0), axis=1, keepdims=True)
    level = lvl_ref[...].astype(F32)
    thermal = trac_ref[0] - 0.6 * trac_ref[1] + 1.5 * ((level + 0.5) / NZ) - 0.5
    factor = fric_ref[...] * thermal
    rows_lane = (iota((ROWS, NZ), 1) % 16 // 4 == iota((ROWS, NZ), 0)).astype(F32)
    contract_first = (((0,), (0,)), ((), ()))
    factor_lanes = lax.dot_general(
        factor, rows_lane, contract_first, precision=lax.Precision.HIGHEST,
        preferred_element_type=F32,
    )
    y_sub = iota((NY, NZ), 0)
    y_lane = iota((NY, NZ), 1)
    in_tile = y_sub % 32 == 4 * (y_lane // 16) + y_lane % 4
    tile_of_y = (iota((NY, RANKS), 0) // 4 == iota((NY, RANKS), 1)).astype(BF16)
    tile_from_y = (iota((RANKS, NY), 1) // 4 == iota((RANKS, NY), 0)).astype(BF16)
    by_tile = mm_exact_left(tile_from_y, jnp.where(in_tile, factor_lanes, 0.0))
    cells = jnp.where(iota((8, RANKS), 0) < cnt_ref[...], list_ref[...], -1).astype(F32)
    slot_spread = (iota((8, 8 * NZ), 1) // NZ == iota((8, 8 * NZ), 0)).astype(F32)
    cell_lanes = lax.dot_general(
        cells, slot_spread, contract_first, preferred_element_type=F32
    )
    position = (lane % 16).astype(F32)
    live = cell_lanes[:, 0:NZ] == position
    for slot in range(1, 8):
        live = jnp.logical_or(live, cell_lanes[:, slot * NZ : (slot + 1) * NZ] == position)
    to_owner = ((me + off) % RANKS == sub).astype(BF16)
    factor_owner = mm_exact_left(to_owner, jnp.where(live, by_tile, 0.0))
    owner_of_y = lax.dot_general(
        tile_of_y, to_owner, (((1,), (1,)), ((), ())), preferred_element_type=F32
    ).astype(BF16)

    def wait_near(stage, ref):
        pltpu.make_async_copy(ref, ref, near_recv.at[stage]).wait()

    wait_near(0, xr.at[pl.ds(0, 3)])
    yr[my_y] = xr[:, my_y]
    for copy in copies_near(
        1, [xr.at[:, y] for y in y_of[1:]], [yr.at[my_y]] * 3, y_peers
    ):
        copy.start()

    modes = modes_ref[...]
    mode_high, mode_low = split(modes)
    scaled_high, scaled_low = split(modes * inv_depth_col)
    spread = (iota((ROWS, ROWS * NZ), 1) // NZ == iota((ROWS, ROWS * NZ), 0)).astype(F32)
    level_lanes = lax.dot_general(
        level, spread, contract_first, preferred_element_type=F32
    )
    for r in range(ROWS):
        hot = (level_lanes[:, r * NZ : (r + 1) * NZ] == y_lane.astype(F32)).astype(BF16)
        wrow[:, r * NZ : (r + 1) * NZ] = mm(hot, scaled_high) + mm(hot, scaled_low)
    loads[0].wait()

    def put_split(field, r):
        high, low = split(field)
        x3[0:NY, r * NZ : (r + 1) * NZ] = high
        x3[NY : 2 * NY, r * NZ : (r + 1) * NZ] = low
        x3[2 * NY : 3 * NY, r * NZ : (r + 1) * NZ] = high

    def divergence(r):
        east, north, up = vel[0, r], vel[1, r], vel[2, r]
        if r > 0:
            east = east - vel[0, r - 1]
        below = jnp.where(y_lane == 0, 0.0, pltpu.roll(up, 1, axis=1))
        flow = east + (north - pltpu.roll(north, 1, axis=0)) + (up - below) * inv_depth
        modal[:, r * NZ : (r + 1) * NZ] = mm3(flow, mode_high, mode_low)

    divergence(0)

    wait_near(1, yr.at[pl.ds(0, 3)])
    for p in range(8):
        for s in range(4):
            ps[p * 16 + s * 4 : p * 16 + s * 4 + 4, :] = yr[s, :, p, :]
    pr[pl.ds(pl.multiple_of(px * 16, 16), 16), :] = ps[pl.ds(pl.multiple_of(px * 16, 16), 16), :]
    for copy in copies_near(
        2,
        [ps.at[pl.ds(pl.multiple_of(p * 16, 16), 16), :] for p in p_of[1:]],
        [pr.at[pl.ds(pl.multiple_of(px * 16, 16), 16), :]] * 7,
        p_peers,
    ):
        copy.start()

    for r in range(1, ROWS):
        divergence(r)
    put_split(mm3(vel[0, ROWS - 1], mode_high, mode_low), ROWS)
    spread_rows = (
        iota((NZ, ROWS * NZ), 0) % 16 // 4 == iota((NZ, ROWS * NZ), 1) // NZ
    ).astype(BF16)

    wait_near(2, pr.at[pl.ds(0, 7 * 16)])
    melt = pr[...] * factor_owner
    s2[pl.ds(8, RANKS, stride=16), :] = melt
    by_y = jnp.where(in_tile, mm_exact_left(owner_of_y, melt), 0.0)
    melt_lanes = mm_exact_right(by_y, spread_rows)
    for r in range(ROWS):
        cols = slice(r * NZ, (r + 1) * NZ)
        put_split(modal[:, cols] + melt_lanes[:, cols] * wrow[:, cols], r)
    for load in loads[1:]:
        load.wait()

    eig = eig_ref[...]

    def block_step(jj, carry):
        rows = pl.ds(pl.multiple_of(jj * BLK, BLK), BLK)
        part = mm(h3[rows, :], x3[...])
        spec[rows, :] = part
        t = 2.0 + (lam_ref[rows, :] + eig)
        u2 = t * t - 1.0
        u3 = t * (t * t - 2.0)
        f = [part[:, r * NZ : (r + 1) * NZ] for r in range(ROWS + 1)]
        s2[pl.ds(2 * jj, RANKS, stride=16), :] = u3 * f[0] + u2 * f[1] + t * f[2] + f[3]
        s2[pl.ds(2 * jj + 1, RANKS, stride=16), :] = f[1] + t * f[2] + u2 * f[3] - u3 * f[4]
        return carry

    lax.fori_loop(0, NB, block_step, 0)

    def send_all(source, target, unit, rows, send_sem, recv_sem):
        def send_row(outer, carry):
            oy, oz = lax.rem(outer, 4), lax.div(outer, 4)
            for dx in range(4):
                qy = lax.rem(my_y + oy + dx, 4)
                pz = lax.rem(my_z + oz + dx, 4)
                for dc in range(2):
                    dest_px = pz * 2 + lax.rem(my_c + dc, 2)
                    dest_py = qy * 4 + x_of[dx]
                    rank = dest_px * 16 + dest_py

                    def send():
                        pltpu.make_async_remote_copy(
                            src_ref=source.at[pl.ds(pl.multiple_of(rank * unit, unit), rows), :],
                            dst_ref=target.at[pl.ds(pl.multiple_of(me * unit, unit), rows), :],
                            send_sem=send_sem,
                            recv_sem=recv_sem,
                            device_id=(dest_px, dest_py),
                            device_id_type=MESH,
                        ).start()

                    if dx == 0 and dc == 0:
                        pl.when(outer > 0)(send)
                    else:
                        send()
            return carry

        lax.fori_loop(0, 16, send_row, 0)
        target[pl.ds(pl.multiple_of(me * unit, unit), rows), :] = source[
            pl.ds(pl.multiple_of(me * unit, unit), rows), :
        ]

    def wait_rows(ref, rows, sem):
        pltpu.make_async_copy(ref.at[pl.ds(0, rows), :], ref.at[pl.ds(0, rows), :], sem).wait()

    send_all(s2, r2, 16, 9, f_send, f_recv)

    t = 2.0 + (lam_ref[...] + eig)
    u2 = t * t - 1.0
    u3 = t * (t * t - 2.0)
    w3 = 1.0 / u3
    w1 = u2 * w3
    w2 = t * w3
    f1, f2, f3 = (spec[:, r * NZ : (r + 1) * NZ] for r in range(1, ROWS))
    modal[:, 0:NZ] = w1 * f1 + w2 * f2 + w3 * f3
    modal[:, NZ : 2 * NZ] = w2 * (f1 + t * f2 + f3)
    modal[:, 2 * NZ : 3 * NZ] = w3 * f1 + w2 * f2 + w1 * f3
    wrow[:, 0:NZ] = w1
    wrow[:, NZ : 2 * NZ] = w2
    wrow[:, 2 * NZ : 3 * NZ] = w3

    for jj in range(4):
        shift = lam_ref[pl.ds(me + jj * RANKS, 1), :] + eig
        edge = 2.0 + shift
        inv[:, jj * NZ : (jj + 1) * NZ] = 1.0 / (
            edge * edge * shift * (4.0 + shift) + lamx_ref[...]
        )
    wait_rows(r2, (RANKS - 1) * 9, f_recv)
    for jj in range(4):
        for h in range(2):
            high, low = split(r2[pl.ds(2 * jj + h, RANKS, stride=16), :])
            for part, value in enumerate((high, low, high)):
                first = part * 2 * RANKS + h * RANKS
                xk[first : first + RANKS, jj * NZ : (jj + 1) * NZ] = value
    solved = mm(hxf_ref[...], xk[...]) * inv[...]
    high, low = split(solved)
    xk[0:RANKS, :] = high
    xk[RANKS : 2 * RANKS, :] = low
    xk[2 * RANKS : 3 * RANKS, :] = high
    both = mm(hxi_ref[...], xk[0 : 3 * RANKS, :])
    for jj in range(4):
        for h in range(2):
            s3[pl.ds(2 * jj + h, RANKS, stride=8), :] = both[
                h * RANKS : (h + 1) * RANKS, jj * NZ : (jj + 1) * NZ
            ]
    send_all(s3, r3, 8, 8, b_send, b_recv)

    pick_got = mm((give == sub).astype(BF16), tile_row)
    thinning = lax.dot_general(
        pick_got, r2[pl.ds(8, RANKS, stride=16), :], contract_first,
        precision=lax.Precision.HIGHEST, preferred_element_type=F32,
    )
    thick_ref[...] = ice_ref[...] - 0.3 * thinning
    synth_high, synth_low = split(synth_ref[...])

    wait_rows(r3, (RANKS - 1) * 8, b_recv)
    for jj in range(4):
        q0 = r3[pl.ds(2 * jj, RANKS, stride=8), :]
        q1 = r3[pl.ds(2 * jj + 1, RANKS, stride=8), :]
        rows = slice(jj * RANKS, (jj + 1) * RANKS)
        w1, w2, w3 = (wrow[rows, r * NZ : (r + 1) * NZ] for r in range(3))
        fields = [
            q0,
            w1 * q0 + w3 * q1 + modal[rows, 0:NZ],
            w2 * (q0 + q1) + modal[rows, NZ : 2 * NZ],
            w3 * q0 + w1 * q1 + modal[rows, 2 * NZ : 3 * NZ],
        ]
        for r in range(ROWS):
            high, low = split(fields[r])
            for part, value in enumerate((high, low, high)):
                first = part * NY + jj * RANKS
                x3[first : first + RANKS, r * NZ : (r + 1) * NZ] = value

    def store_of(block):
        rows = pl.ds(pl.multiple_of(block * BLK, BLK), BLK)
        return pltpu.make_async_copy(outv.at[:, rows], out_hbm.at[:, rows], out_sem.at[block])

    def out_step(block, carry):
        rows = pl.ds(pl.multiple_of(block * BLK, BLK), BLK)
        part = mm(h3[rows, :], x3[:, 0 : ROWS * NZ])
        for r in range(ROWS):
            outv[r, rows, :] = mm3(part[:, r * NZ : (r + 1) * NZ], synth_high, synth_low)
        store_of(block).start()
        return carry

    lax.fori_loop(0, NB, out_step, 0)
    pltpu.make_async_copy(xr.at[pl.ds(0, 3)], xr.at[pl.ds(0, 3)], near_send.at[0]).wait()
    pltpu.make_async_copy(yr.at[pl.ds(0, 3)], yr.at[pl.ds(0, 3)], near_send.at[1]).wait()
    wait_rows(ps, 7 * 16, near_send.at[2])
    wait_rows(s2, (RANKS - 1) * 9, f_send)
    wait_rows(s3, (RANKS - 1) * 8, b_send)
    for block in range(NB):
        store_of(block).wait()


def body(
    velocity,
    layer_depth,
    vertical_modes,
    vertical_synthesis,
    mode_eigen,
    boundary_tracers,
    friction_speed,
    draft_level,
    tile_offset,
    draft_count,
    draft_list,
    exchange_coeff,
    ice_thickness,
):
    hh, hl = split_table(hartley(NY))
    small = hartley(RANKS)
    following = (np.arange(RANKS) + 1) % RANKS
    fwd_high, fwd_low = split_table(np.concatenate([small, small[:, following]], axis=1))
    inv_high, inv_low = split_table(np.concatenate([small, small[following]], axis=0))
    hxf = np.concatenate([fwd_high, fwd_high, fwd_low], axis=1)
    hxi = np.concatenate([inv_high, inv_high, inv_low], axis=1)
    lam = np.repeat(eigen(NY)[:, None], NZ, axis=1).astype(np.float32)
    lamx = np.repeat(eigen(RANKS)[:, None], NZ, axis=1).astype(np.float32)
    vmem = pl.BlockSpec(memory_space=pltpu.VMEM)
    hbm = pl.BlockSpec(memory_space=pl.ANY)
    tiles = (RANKS * 8, NZ)
    pressure, thickness = pl.pallas_call(
        kernel,
        out_shape=(
            jax.ShapeDtypeStruct((ROWS, NY, NZ), F32),
            jax.ShapeDtypeStruct((16, 128), F32),
        ),
        in_specs=[hbm] * 3 + [vmem] * 16,
        out_specs=(hbm, vmem),
        scratch_shapes=[
            pltpu.VMEM((3, ROWS, NY, NZ), F32),
            pltpu.VMEM((NY, 3 * NY), BF16),
            pltpu.VMEM((3 * NY, (ROWS + 1) * NZ), BF16),
            pltpu.VMEM((NY, ROWS * NZ), F32),
            pltpu.VMEM((NY, (ROWS + 1) * NZ), F32),
            pltpu.VMEM((NY, ROWS * NZ), F32),
            pltpu.VMEM((ROWS, NY, NZ), F32),
            pltpu.VMEM((6 * RANKS, 4 * NZ), BF16),
            pltpu.VMEM((RANKS, 4 * NZ), F32),
            pltpu.VMEM((4, 4, 8, NZ), F32),
            pltpu.VMEM((4, 4, 8, NZ), F32),
            pltpu.VMEM((4, 4, 8, NZ), F32),
            pltpu.VMEM((RANKS, NZ), F32),
            pltpu.VMEM((RANKS, NZ), F32),
            pltpu.VMEM((RANKS * 16, NZ), F32),
            pltpu.VMEM((RANKS * 16, NZ), F32),
            pltpu.VMEM((RANKS * 8, NZ), F32),
            pltpu.VMEM((RANKS * 8, NZ), F32),
            pltpu.SemaphoreType.DMA((4,)),
            pltpu.SemaphoreType.DMA((NB,)),
            pltpu.SemaphoreType.DMA((3,)),
            pltpu.SemaphoreType.DMA((3,)),
            pltpu.SemaphoreType.DMA,
            pltpu.SemaphoreType.DMA,
            pltpu.SemaphoreType.DMA,
            pltpu.SemaphoreType.DMA,
        ],
        compiler_params=pltpu.CompilerParams(
            collective_id=0, has_side_effects=True, vmem_limit_bytes=56 * 2**20
        ),
    )(
        velocity,
        hh,
        hl,
        hxf,
        hxi,
        lam,
        lamx,
        layer_depth.reshape(1, NZ),
        vertical_modes,
        vertical_synthesis,
        mode_eigen.reshape(1, NZ),
        boundary_tracers,
        friction_speed,
        draft_level,
        tile_offset.reshape(1, RANKS),
        draft_count,
        jnp.swapaxes(draft_list, 1, 2).reshape(8, RANKS),
        exchange_coeff.reshape(16, 128),
        ice_thickness.reshape(16, 128),
    )
    return (pressure, thickness.reshape(2048))


def solution(mesh):
    in_specs = (
        P(None, ("px", "py"), None, None),
        P(),
        P(),
        P(),
        P(),
        P(None, ("px", "py"), None),
        P(("px", "py"), None),
        P(("px", "py"), None),
        P(),
        P(("px", "py"), None),
        P(("px", "py"), None, None),
        P(("px", "py")),
        P(("px", "py")),
    )
    out_specs = (P(("px", "py"), None, None), P(("px", "py")))
    return jax.shard_map(body, mesh=mesh, in_specs=in_specs, out_specs=out_specs, check_vma=False)
```

```python
import math
import random

import jax
import jax.numpy as jnp
import numpy as np
from jax import lax
from jax.experimental import pallas as pl
from jax.experimental.pallas import tpu as pltpu
from jax.sharding import PartitionSpec as P

NX = 512
NY = 512
NZ = 128
RANKS = 128
ROWS = 4
NB = 4
BLK = NY // NB
MESH = pl.DeviceIdType.MESH
F32 = jnp.float32
BF16 = jnp.bfloat16


def hops(offset):
    dz, dy, dx, dc = offset
    return sum(min(d, 4 - d) for d in (dz, dy, dx))


def farthest_first(dzs):
    offsets = [
        (dz, dy, dx, dc)
        for dz in dzs
        for dy in range(4)
        for dx in range(4)
        for dc in range(2)
        if (dz, dy, dx, dc) != (0, 0, 0, 0)
    ]
    random.Random(2).shuffle(offsets)
    return sorted(offsets, key=lambda offset: -hops(offset))


def hartley(length):
    index = np.arange(length)
    angle = (np.outer(index, index) % length) * (2.0 * math.pi / length)
    return (np.cos(angle) + np.sin(angle)) / math.sqrt(length)


def split_table(table):
    high = np.asarray(table, np.float32).astype(jnp.bfloat16)
    low = (np.asarray(table, np.float32) - high.astype(np.float32)).astype(jnp.bfloat16)
    return high, low


def eigen(length):
    return 2.0 - 2.0 * np.cos(2.0 * math.pi * np.arange(length) / length)


def split(x):
    high = x.astype(BF16)
    return high, (x - high.astype(F32)).astype(BF16)


def mm(a, b):
    return jnp.dot(a, b, preferred_element_type=F32)


def mm_exact_left(a, x):
    high, low = split(x)
    return mm(a, high) + mm(a, low)


def mm_exact_right(x, b):
    high, low = split(x)
    return mm(high, b) + mm(low, b)


def mm3(x, b_high, b_low):
    high, low = split(x)
    return mm(high, b_high) + mm(low, b_high) + mm(high, b_low)


def iota(shape, axis):
    return lax.broadcasted_iota(jnp.int32, shape, axis)


def kernel(
    vel_hbm,
    hh_hbm,
    hl_hbm,
    hxf_ref,
    hxi_ref,
    lam_ref,
    lamx_ref,
    depth_ref,
    modes_ref,
    synth_ref,
    eig_ref,
    trac_ref,
    fric_ref,
    lvl_ref,
    off_ref,
    cnt_ref,
    list_ref,
    coeff_ref,
    ice_ref,
    out_hbm,
    thick_ref,
    vel,
    h3,
    x3,
    modal,
    spec,
    wrow,
    outv,
    xk,
    inv,
    xs,
    xr,
    s2,
    r2,
    s3,
    r3,
    load_sem,
    out_sem,
    c_send,
    c_recv,
    f_send,
    f_recv,
    b_send,
    b_recv,
):
    px = lax.axis_index("px")
    py = lax.axis_index("py")
    my_z, my_c, my_y, my_x = px // 2, px % 2, py // 4, py % 4
    me = px * 16 + py

    loads = [pltpu.make_async_copy(vel_hbm, vel, load_sem.at[0])]
    for part, table in enumerate((hh_hbm, hh_hbm, hl_hbm)):
        loads.append(
            pltpu.make_async_copy(
                table, h3.at[:, pl.ds(part * NY, NY)], load_sem.at[1 + part]
            )
        )
    for load in loads:
        load.start()

    z_of = [(my_z + d) % 4 for d in range(4)]
    c_of = [my_c, 1 - my_c]
    px_of = [[z_of[dz] * 2 + c_of[dc] for dc in range(2)] for dz in range(4)]
    py_of = [[(my_y + dy) % 4 * 4 + (my_x + dx) % 4 for dx in range(4)] for dy in range(4)]
    everyone = farthest_first(range(4))
    barrier = pltpu.get_barrier_semaphore()
    for dz, dy, dx, dc in everyone:
        pl.semaphore_signal(
            barrier, inc=1, device_id=(px_of[dz][dc], py_of[dy][dx]), device_id_type=MESH
        )

    off = off_ref[...]
    sub = iota((RANKS, RANKS), 0)
    lane = iota((RANKS, RANKS), 1)
    tile_row = (iota((RANKS, 16), 0) // 8 == iota((RANKS, 16), 1)).astype(BF16)
    pick = mm(((me - off + RANKS) % RANKS == sub).astype(BF16), tile_row)
    xs[pl.ds(0, RANKS, stride=8), :] = jnp.dot(
        pick, coeff_ref[...], precision=lax.Precision.HIGHEST
    )

    def send_all(offsets, source, target, unit, rows, send_sem, recv_sem):
        for dz, dy, dx, dc in offsets:
            dest_px, dest_py = px_of[dz][dc], py_of[dy][dx]
            first = pl.multiple_of((dest_px * 16 + dest_py) * unit, unit)
            pltpu.make_async_remote_copy(
                src_ref=source.at[pl.ds(first, rows), :],
                dst_ref=target.at[pl.ds(pl.multiple_of(me * unit, unit), rows), :],
                send_sem=send_sem,
                recv_sem=recv_sem,
                device_id=(dest_px, dest_py),
                device_id_type=MESH,
            ).start()

    def keep_own(source, target, unit, rows):
        own = pl.ds(pl.multiple_of(me * unit, unit), rows)
        target[own, :] = source[own, :]

    def wait_rows(ref, rows, sem):
        pltpu.make_async_copy(ref.at[pl.ds(0, rows), :], ref.at[pl.ds(0, rows), :], sem).wait()

    pl.semaphore_wait(barrier, RANKS - 1)
    send_all(everyone, xs, xr, 8, 1, c_send, c_recv)
    keep_own(xs, xr, 8, 1)

    inv_depth = 1.0 / depth_ref[...]
    inv_depth_col = jnp.sum(jnp.where(sub == lane, inv_depth, 0.0), axis=1, keepdims=True)
    level = lvl_ref[...].astype(F32)
    thermal = trac_ref[0] - 0.6 * trac_ref[1] + 1.5 * ((level + 0.5) / NZ) - 0.5
    factor = fric_ref[...] * thermal
    rows_lane = (iota((ROWS, NZ), 1) % 16 // 4 == iota((ROWS, NZ), 0)).astype(F32)
    contract_first = (((0,), (0,)), ((), ()))
    factor_lanes = lax.dot_general(
        factor, rows_lane, contract_first, precision=lax.Precision.HIGHEST,
        preferred_element_type=F32,
    )
    y_sub = iota((NY, NZ), 0)
    y_lane = iota((NY, NZ), 1)
    in_tile = y_sub % 32 == 4 * (y_lane // 16) + y_lane % 4
    tile_of_y = (iota((NY, RANKS), 0) // 4 == iota((NY, RANKS), 1)).astype(BF16)
    tile_from_y = (iota((RANKS, NY), 1) // 4 == iota((RANKS, NY), 0)).astype(BF16)
    by_tile = mm_exact_left(tile_from_y, jnp.where(in_tile, factor_lanes, 0.0))
    cells = jnp.where(iota((8, RANKS), 0) < cnt_ref[...], list_ref[...], -1).astype(F32)
    slot_spread = (iota((8, 8 * NZ), 1) // NZ == iota((8, 8 * NZ), 0)).astype(F32)
    cell_lanes = lax.dot_general(
        cells, slot_spread, contract_first, preferred_element_type=F32
    )
    position = (lane % 16).astype(F32)
    live = cell_lanes[:, 0:NZ] == position
    for slot in range(1, 8):
        live = jnp.logical_or(live, cell_lanes[:, slot * NZ : (slot + 1) * NZ] == position)
    to_owner = ((me + off) % RANKS == sub).astype(BF16)
    factor_owner = mm_exact_left(to_owner, jnp.where(live, by_tile, 0.0))
    owner_of_y = lax.dot_general(
        tile_of_y, to_owner, (((1,), (1,)), ((), ())), preferred_element_type=F32
    ).astype(BF16)

    modes = modes_ref[...]
    mode_high, mode_low = split(modes)
    scaled_high, scaled_low = split(modes * inv_depth_col)
    spread = (iota((ROWS, ROWS * NZ), 1) // NZ == iota((ROWS, ROWS * NZ), 0)).astype(F32)
    level_lanes = lax.dot_general(
        level, spread, contract_first, preferred_element_type=F32
    )
    for r in range(ROWS):
        hot = (level_lanes[:, r * NZ : (r + 1) * NZ] == y_lane.astype(F32)).astype(BF16)
        wrow[:, r * NZ : (r + 1) * NZ] = mm(hot, scaled_high) + mm(hot, scaled_low)
    loads[0].wait()

    def put_split(field, r):
        high, low = split(field)
        x3[0:NY, r * NZ : (r + 1) * NZ] = high
        x3[NY : 2 * NY, r * NZ : (r + 1) * NZ] = low
        x3[2 * NY : 3 * NY, r * NZ : (r + 1) * NZ] = high

    def divergence(r):
        east, north, up = vel[0, r], vel[1, r], vel[2, r]
        if r > 0:
            east = east - vel[0, r - 1]
        below = jnp.where(y_lane == 0, 0.0, pltpu.roll(up, 1, axis=1))
        flow = east + (north - pltpu.roll(north, 1, axis=0)) + (up - below) * inv_depth
        modal[:, r * NZ : (r + 1) * NZ] = mm3(flow, mode_high, mode_low)

    for r in range(ROWS):
        divergence(r)
    put_split(mm3(vel[0, ROWS - 1], mode_high, mode_low), ROWS)
    spread_rows = (
        iota((NZ, ROWS * NZ), 0) % 16 // 4 == iota((NZ, ROWS * NZ), 1) // NZ
    ).astype(BF16)

    wait_rows(xr, RANKS - 1, c_recv)
    melt = xr[pl.ds(0, RANKS, stride=8), :] * factor_owner
    s2[pl.ds(8, RANKS, stride=16), :] = melt
    by_y = jnp.where(in_tile, mm_exact_left(owner_of_y, melt), 0.0)
    melt_lanes = mm_exact_right(by_y, spread_rows)
    for r in range(ROWS):
        cols = slice(r * NZ, (r + 1) * NZ)
        put_split(modal[:, cols] + melt_lanes[:, cols] * wrow[:, cols], r)
    for load in loads[1:]:
        load.wait()

    eig = eig_ref[...]

    for dz in (2, 1, 3, 0):
        rows = pl.ds(pl.multiple_of(z_of[dz] * BLK, BLK), BLK)
        part = mm(h3[rows, :], x3[...])
        spec[rows, :] = part
        t = 2.0 + (lam_ref[rows, :] + eig)
        u2 = t * t - 1.0
        u3 = t * (t * t - 2.0)
        f = [part[:, r * NZ : (r + 1) * NZ] for r in range(ROWS + 1)]
        first = u3 * f[0] + u2 * f[1] + t * f[2] + f[3]
        second = f[1] + t * f[2] + u2 * f[3] - u3 * f[4]
        start = pl.multiple_of(z_of[dz] * 512, 512)
        for jj in range(4):
            own = slice(jj * 32, (jj + 1) * 32)
            s2[pl.ds(start + 2 * jj, 32, stride=16), :] = first[own]
            s2[pl.ds(start + 2 * jj + 1, 32, stride=16), :] = second[own]
        send_all(farthest_first([dz]), s2, r2, 16, 9, f_send, f_recv)
    keep_own(s2, r2, 16, 9)

    t = 2.0 + (lam_ref[...] + eig)
    u2 = t * t - 1.0
    u3 = t * (t * t - 2.0)
    w3 = 1.0 / u3
    w1 = u2 * w3
    w2 = t * w3
    f1, f2, f3 = (spec[:, r * NZ : (r + 1) * NZ] for r in range(1, ROWS))
    modal[:, 0:NZ] = w1 * f1 + w2 * f2 + w3 * f3
    modal[:, NZ : 2 * NZ] = w2 * (f1 + t * f2 + f3)
    modal[:, 2 * NZ : 3 * NZ] = w3 * f1 + w2 * f2 + w1 * f3
    wrow[:, 0:NZ] = w1
    wrow[:, NZ : 2 * NZ] = w2
    wrow[:, 2 * NZ : 3 * NZ] = w3

    for jj in range(4):
        shift = lam_ref[pl.ds(my_z * 128 + jj * 32 + (me - my_z * 32), 1), :] + eig
        edge = 2.0 + shift
        inv[:, jj * NZ : (jj + 1) * NZ] = 1.0 / (
            edge * edge * shift * (4.0 + shift) + lamx_ref[...]
        )
    wait_rows(r2, (RANKS - 1) * 9, f_recv)
    for jj in range(4):
        for h in range(2):
            high, low = split(r2[pl.ds(2 * jj + h, RANKS, stride=16), :])
            for part, value in enumerate((high, low, high)):
                first = part * 2 * RANKS + h * RANKS
                xk[first : first + RANKS, jj * NZ : (jj + 1) * NZ] = value
    solved = mm(hxf_ref[...], xk[...]) * inv[...]
    high, low = split(solved)
    xk[0:RANKS, :] = high
    xk[RANKS : 2 * RANKS, :] = low
    xk[2 * RANKS : 3 * RANKS, :] = high
    both = mm(hxi_ref[...], xk[0 : 3 * RANKS, :])
    for jj in range(4):
        for h in range(2):
            s3[pl.ds(2 * jj + h, RANKS, stride=8), :] = both[
                h * RANKS : (h + 1) * RANKS, jj * NZ : (jj + 1) * NZ
            ]
    send_all(everyone, s3, r3, 8, 8, b_send, b_recv)
    keep_own(s3, r3, 8, 8)

    thinning = lax.dot_general(
        pick, r2[pl.ds(8, RANKS, stride=16), :], contract_first,
        precision=lax.Precision.HIGHEST, preferred_element_type=F32,
    )
    thick_ref[...] = ice_ref[...] - 0.3 * thinning
    synth_high, synth_low = split(synth_ref[...])

    wait_rows(r3, (RANKS - 1) * 8, b_recv)
    for z in range(4):
        for jj in range(4):
            q0 = r3[pl.ds(z * 256 + 2 * jj, 32, stride=8), :]
            q1 = r3[pl.ds(z * 256 + 2 * jj + 1, 32, stride=8), :]
            rows = slice(z * 128 + jj * 32, z * 128 + (jj + 1) * 32)
            w1, w2, w3 = (wrow[rows, r * NZ : (r + 1) * NZ] for r in range(3))
            fields = [
                q0,
                w1 * q0 + w3 * q1 + modal[rows, 0:NZ],
                w2 * (q0 + q1) + modal[rows, NZ : 2 * NZ],
                w3 * q0 + w1 * q1 + modal[rows, 2 * NZ : 3 * NZ],
            ]
            for r in range(ROWS):
                high, low = split(fields[r])
                for part, value in enumerate((high, low, high)):
                    first = part * NY + z * 128 + jj * 32
                    x3[first : first + 32, r * NZ : (r + 1) * NZ] = value

    def store_of(block):
        rows = pl.ds(pl.multiple_of(block * BLK, BLK), BLK)
        return pltpu.make_async_copy(outv.at[:, rows], out_hbm.at[:, rows], out_sem.at[block])

    def out_step(block, carry):
        rows = pl.ds(pl.multiple_of(block * BLK, BLK), BLK)
        part = mm(h3[rows, :], x3[:, 0 : ROWS * NZ])
        for r in range(ROWS):
            outv[r, rows, :] = mm3(part[:, r * NZ : (r + 1) * NZ], synth_high, synth_low)
        store_of(block).start()
        return carry

    lax.fori_loop(0, NB, out_step, 0)
    wait_rows(xs, RANKS - 1, c_send)
    wait_rows(s2, (RANKS - 1) * 9, f_send)
    wait_rows(s3, (RANKS - 1) * 8, b_send)
    for block in range(NB):
        store_of(block).wait()


def body(
    velocity,
    layer_depth,
    vertical_modes,
    vertical_synthesis,
    mode_eigen,
    boundary_tracers,
    friction_speed,
    draft_level,
    tile_offset,
    draft_count,
    draft_list,
    exchange_coeff,
    ice_thickness,
):
    hh, hl = split_table(hartley(NY))
    small = hartley(RANKS)
    following = (np.arange(RANKS) + 1) % RANKS
    fwd_high, fwd_low = split_table(np.concatenate([small, small[:, following]], axis=1))
    inv_high, inv_low = split_table(np.concatenate([small, small[following]], axis=0))
    hxf = np.concatenate([fwd_high, fwd_high, fwd_low], axis=1)
    hxi = np.concatenate([inv_high, inv_high, inv_low], axis=1)
    lam = np.repeat(eigen(NY)[:, None], NZ, axis=1).astype(np.float32)
    lamx = np.repeat(eigen(RANKS)[:, None], NZ, axis=1).astype(np.float32)
    vmem = pl.BlockSpec(memory_space=pltpu.VMEM)
    hbm = pl.BlockSpec(memory_space=pl.ANY)
    tiles = (RANKS * 8, NZ)
    pressure, thickness = pl.pallas_call(
        kernel,
        out_shape=(
            jax.ShapeDtypeStruct((ROWS, NY, NZ), F32),
            jax.ShapeDtypeStruct((16, 128), F32),
        ),
        in_specs=[hbm] * 3 + [vmem] * 16,
        out_specs=(hbm, vmem),
        scratch_shapes=[
            pltpu.VMEM((3, ROWS, NY, NZ), F32),
            pltpu.VMEM((NY, 3 * NY), BF16),
            pltpu.VMEM((3 * NY, (ROWS + 1) * NZ), BF16),
            pltpu.VMEM((NY, ROWS * NZ), F32),
            pltpu.VMEM((NY, (ROWS + 1) * NZ), F32),
            pltpu.VMEM((NY, ROWS * NZ), F32),
            pltpu.VMEM((ROWS, NY, NZ), F32),
            pltpu.VMEM((6 * RANKS, 4 * NZ), BF16),
            pltpu.VMEM((RANKS, 4 * NZ), F32),
            pltpu.VMEM((RANKS * 8, NZ), F32),
            pltpu.VMEM((RANKS * 8, NZ), F32),
            pltpu.VMEM((RANKS * 16, NZ), F32),
            pltpu.VMEM((RANKS * 16, NZ), F32),
            pltpu.VMEM((RANKS * 8, NZ), F32),
            pltpu.VMEM((RANKS * 8, NZ), F32),
            pltpu.SemaphoreType.DMA((4,)),
            pltpu.SemaphoreType.DMA((NB,)),
            pltpu.SemaphoreType.DMA,
            pltpu.SemaphoreType.DMA,
            pltpu.SemaphoreType.DMA,
            pltpu.SemaphoreType.DMA,
            pltpu.SemaphoreType.DMA,
            pltpu.SemaphoreType.DMA,
        ],
        compiler_params=pltpu.CompilerParams(
            collective_id=0, has_side_effects=True, vmem_limit_bytes=56 * 2**20
        ),
    )(
        velocity,
        hh,
        hl,
        hxf,
        hxi,
        lam,
        lamx,
        layer_depth.reshape(1, NZ),
        vertical_modes,
        vertical_synthesis,
        mode_eigen.reshape(1, NZ),
        boundary_tracers,
        friction_speed,
        draft_level,
        tile_offset.reshape(1, RANKS),
        draft_count,
        jnp.swapaxes(draft_list, 1, 2).reshape(8, RANKS),
        exchange_coeff.reshape(16, 128),
        ice_thickness.reshape(16, 128),
    )
    return (pressure, thickness.reshape(2048))


def solution(mesh):
    in_specs = (
        P(None, ("px", "py"), None, None),
        P(),
        P(),
        P(),
        P(),
        P(None, ("px", "py"), None),
        P(("px", "py"), None),
        P(("px", "py"), None),
        P(),
        P(("px", "py"), None),
        P(("px", "py"), None, None),
        P(("px", "py")),
        P(("px", "py")),
    )
    out_specs = (P(("px", "py"), None, None), P(("px", "py")))
    return jax.shard_map(body, mesh=mesh, in_specs=in_specs, out_specs=out_specs, check_vma=False)
```

```python
import math
import random

import jax
import jax.numpy as jnp
import numpy as np
from jax import lax
from jax.experimental import pallas as pl
from jax.experimental.pallas import tpu as pltpu
from jax.sharding import PartitionSpec as P

NX = 512
NY = 512
NZ = 128
RANKS = 128
ROWS = 4
NB = 4
BLK = NY // NB
MESH = pl.DeviceIdType.MESH
F32 = jnp.float32
BF16 = jnp.bfloat16


def hops(offset):
    dz, dy, dx, dc = offset
    return sum(min(d, 4 - d) for d in (dz, dy, dx))


def farthest_first(dzs):
    offsets = [
        (dz, dy, dx, dc)
        for dz in dzs
        for dy in range(4)
        for dx in range(4)
        for dc in range(2)
        if (dz, dy, dx, dc) != (0, 0, 0, 0)
    ]
    random.Random(2).shuffle(offsets)
    return sorted(offsets, key=lambda offset: -hops(offset))


def hartley(length):
    index = np.arange(length)
    angle = (np.outer(index, index) % length) * (2.0 * math.pi / length)
    return (np.cos(angle) + np.sin(angle)) / math.sqrt(length)


def split_table(table):
    high = np.asarray(table, np.float32).astype(jnp.bfloat16)
    low = (np.asarray(table, np.float32) - high.astype(np.float32)).astype(jnp.bfloat16)
    return high, low


def eigen(length):
    return 2.0 - 2.0 * np.cos(2.0 * math.pi * np.arange(length) / length)


def split(x):
    high = x.astype(BF16)
    return high, (x - high.astype(F32)).astype(BF16)


def mm(a, b):
    return jnp.dot(a, b, preferred_element_type=F32)


def mm_exact_left(a, x):
    high, low = split(x)
    return mm(a, high) + mm(a, low)


def mm_exact_right(x, b):
    high, low = split(x)
    return mm(high, b) + mm(low, b)


def mm3(x, b_high, b_low):
    high, low = split(x)
    return mm(high, b_high) + mm(low, b_high) + mm(high, b_low)


def iota(shape, axis):
    return lax.broadcasted_iota(jnp.int32, shape, axis)


def kernel(
    vel_hbm,
    hh_hbm,
    hl_hbm,
    hxf_hbm,
    hxi_hbm,
    lam_hbm,
    lamx_hbm,
    depth_hbm,
    modes_hbm,
    synth_hbm,
    ice_hbm,
    eig_hbm,
    trac_hbm,
    fric_hbm,
    lvl_hbm,
    off_hbm,
    cnt_hbm,
    list_hbm,
    coeff_hbm,
    out_hbm,
    thick_ref,
    hxf_ref,
    hxi_ref,
    lam_ref,
    lamx_ref,
    depth_ref,
    modes_ref,
    synth_ref,
    ice_ref,
    eig_ref,
    trac_ref,
    fric_ref,
    lvl_ref,
    off_ref,
    cnt_ref,
    list_ref,
    coeff_ref,
    vel,
    h3,
    x3,
    modal,
    spec,
    wrow,
    xk,
    inv,
    xs,
    xr,
    s2,
    r2,
    s3,
    r3,
    hb,
    acc,
    outv,
    load_sem,
    out_sem,
    c_send,
    c_recv,
    f_send,
    f_recv,
    b_send,
    b_recv,
):
    px = lax.axis_index("px")
    py = lax.axis_index("py")
    my_z, my_c, my_y, my_x = px // 2, px % 2, py // 4, py % 4
    me = px * 16 + py

    def load(source, target, index):
        return pltpu.make_async_copy(source, target, load_sem.at[index])

    small = [
        load(source, target, index)
        for index, (source, target) in enumerate(
            (
                (off_hbm, off_ref),
                (coeff_hbm, coeff_ref),
                (trac_hbm, trac_ref),
                (fric_hbm, fric_ref),
                (lvl_hbm, lvl_ref),
                (cnt_hbm, cnt_ref),
                (list_hbm, list_ref),
                (depth_hbm, depth_ref),
                (modes_hbm, modes_ref),
                (eig_hbm, eig_ref),
            )
        )
    ]
    large = [
        load(source, target, index + len(small))
        for index, (source, target) in enumerate(
            (
                (vel_hbm, vel),
                (hh_hbm, h3.at[:, pl.ds(0, NY)]),
                (hh_hbm, h3.at[:, pl.ds(NY, NY)]),
                (hl_hbm, h3.at[:, pl.ds(2 * NY, NY)]),
                (lam_hbm, lam_ref),
                (lamx_hbm, lamx_ref),
                (hxf_hbm, hxf_ref),
                (hxi_hbm, hxi_ref),
                (synth_hbm, synth_ref),
                (ice_hbm, ice_ref),
            )
            + tuple(
                (
                    table.at[:, pl.ds(b * BLK, BLK)],
                    hb.at[b, :, pl.ds(part * BLK, BLK)],
                )
                for b in range(NB)
                for part, table in enumerate((hh_hbm, hh_hbm, hl_hbm))
            )
        )
    ]

    z_of = [(my_z + d) % 4 for d in range(4)]
    c_of = [my_c, 1 - my_c]
    px_of = [[z_of[dz] * 2 + c_of[dc] for dc in range(2)] for dz in range(4)]
    py_of = [[(my_y + dy) % 4 * 4 + (my_x + dx) % 4 for dx in range(4)] for dy in range(4)]
    everyone = farthest_first(range(4))
    barrier = pltpu.get_barrier_semaphore()
    for dz, dy, dx, dc in everyone:
        pl.semaphore_signal(
            barrier, inc=1, device_id=(px_of[dz][dc], py_of[dy][dx]), device_id_type=MESH
        )

    for copy in small + large:
        copy.start()
    for copy in small:
        copy.wait()

    off = off_ref[...]
    sub = iota((RANKS, RANKS), 0)
    lane = iota((RANKS, RANKS), 1)
    tile_row = (iota((RANKS, 16), 0) // 8 == iota((RANKS, 16), 1)).astype(BF16)
    pick = mm(((me - off + RANKS) % RANKS == sub).astype(BF16), tile_row)
    xs[pl.ds(0, RANKS, stride=8), :] = jnp.dot(
        pick, coeff_ref[...], precision=lax.Precision.HIGHEST
    )

    def send_all(offsets, source, target, unit, rows, send_sem, recv_sem):
        for dz, dy, dx, dc in offsets:
            dest_px, dest_py = px_of[dz][dc], py_of[dy][dx]
            first = pl.multiple_of((dest_px * 16 + dest_py) * unit, unit)
            pltpu.make_async_remote_copy(
                src_ref=source.at[pl.ds(first, rows), :],
                dst_ref=target.at[pl.ds(pl.multiple_of(me * unit, unit), rows), :],
                send_sem=send_sem,
                recv_sem=recv_sem,
                device_id=(dest_px, dest_py),
                device_id_type=MESH,
            ).start()

    def keep_own(source, target, unit, rows):
        own = pl.ds(pl.multiple_of(me * unit, unit), rows)
        target[own, :] = source[own, :]

    def wait_rows(ref, rows, sem):
        pltpu.make_async_copy(ref.at[pl.ds(0, rows), :], ref.at[pl.ds(0, rows), :], sem).wait()

    pl.semaphore_wait(barrier, RANKS - 1)
    send_all(everyone, xs, xr, 8, 1, c_send, c_recv)
    keep_own(xs, xr, 8, 1)

    inv_depth = 1.0 / depth_ref[...]
    inv_depth_col = jnp.sum(jnp.where(sub == lane, inv_depth, 0.0), axis=1, keepdims=True)
    level = lvl_ref[...].astype(F32)
    thermal = trac_ref[0] - 0.6 * trac_ref[1] + 1.5 * ((level + 0.5) / NZ) - 0.5
    factor = fric_ref[...] * thermal
    rows_lane = (iota((ROWS, NZ), 1) % 16 // 4 == iota((ROWS, NZ), 0)).astype(F32)
    contract_first = (((0,), (0,)), ((), ()))
    factor_lanes = lax.dot_general(
        factor, rows_lane, contract_first, precision=lax.Precision.HIGHEST,
        preferred_element_type=F32,
    )
    y_sub = iota((NY, NZ), 0)
    y_lane = iota((NY, NZ), 1)
    in_tile = y_sub % 32 == 4 * (y_lane // 16) + y_lane % 4
    tile_of_y = (iota((NY, RANKS), 0) // 4 == iota((NY, RANKS), 1)).astype(BF16)
    tile_from_y = (iota((RANKS, NY), 1) // 4 == iota((RANKS, NY), 0)).astype(BF16)
    by_tile = mm_exact_left(tile_from_y, jnp.where(in_tile, factor_lanes, 0.0))
    cells = jnp.where(iota((8, RANKS), 0) < cnt_ref[...], list_ref[...], -1).astype(F32)
    slot_spread = (iota((8, 8 * NZ), 1) // NZ == iota((8, 8 * NZ), 0)).astype(F32)
    cell_lanes = lax.dot_general(
        cells, slot_spread, contract_first, preferred_element_type=F32
    )
    position = (lane % 16).astype(F32)
    live = cell_lanes[:, 0:NZ] == position
    for slot in range(1, 8):
        live = jnp.logical_or(live, cell_lanes[:, slot * NZ : (slot + 1) * NZ] == position)
    to_owner = ((me + off) % RANKS == sub).astype(BF16)
    factor_owner = mm_exact_left(to_owner, jnp.where(live, by_tile, 0.0))
    owner_of_y = lax.dot_general(
        tile_of_y, to_owner, (((1,), (1,)), ((), ())), preferred_element_type=F32
    ).astype(BF16)

    modes = modes_ref[...]
    mode_high, mode_low = split(modes)
    scaled_high, scaled_low = split(modes * inv_depth_col)
    spread = (iota((ROWS, ROWS * NZ), 1) // NZ == iota((ROWS, ROWS * NZ), 0)).astype(F32)
    level_lanes = lax.dot_general(
        level, spread, contract_first, preferred_element_type=F32
    )
    for r in range(ROWS):
        hot = (level_lanes[:, r * NZ : (r + 1) * NZ] == y_lane.astype(F32)).astype(BF16)
        wrow[:, r * NZ : (r + 1) * NZ] = mm(hot, scaled_high) + mm(hot, scaled_low)
    large[0].wait()

    def put_split(field, r):
        high, low = split(field)
        x3[0:NY, r * NZ : (r + 1) * NZ] = high
        x3[NY : 2 * NY, r * NZ : (r + 1) * NZ] = low
        x3[2 * NY : 3 * NY, r * NZ : (r + 1) * NZ] = high

    def divergence(r):
        east, north, up = vel[0, r], vel[1, r], vel[2, r]
        if r > 0:
            east = east - vel[0, r - 1]
        below = jnp.where(y_lane == 0, 0.0, pltpu.roll(up, 1, axis=1))
        flow = east + (north - pltpu.roll(north, 1, axis=0)) + (up - below) * inv_depth
        modal[:, r * NZ : (r + 1) * NZ] = mm3(flow, mode_high, mode_low)

    for r in range(ROWS):
        divergence(r)
    put_split(mm3(vel[0, ROWS - 1], mode_high, mode_low), ROWS)
    for copy in large[1:6]:
        copy.wait()
    spec[:, ROWS * NZ : (ROWS + 1) * NZ] = mm(h3[...], x3[:, ROWS * NZ : (ROWS + 1) * NZ])
    spread_rows = (
        iota((NZ, ROWS * NZ), 0) % 16 // 4 == iota((NZ, ROWS * NZ), 1) // NZ
    ).astype(BF16)

    wait_rows(xr, RANKS - 1, c_recv)
    melt = xr[pl.ds(0, RANKS, stride=8), :] * factor_owner
    s2[pl.ds(8, RANKS, stride=16), :] = melt
    by_y = jnp.where(in_tile, mm_exact_left(owner_of_y, melt), 0.0)
    melt_lanes = mm_exact_right(by_y, spread_rows)
    for r in range(ROWS):
        cols = slice(r * NZ, (r + 1) * NZ)
        put_split(modal[:, cols] + melt_lanes[:, cols] * wrow[:, cols], r)

    eig = eig_ref[...]

    for dz in (2, 1, 3, 0):
        rows = pl.ds(pl.multiple_of(z_of[dz] * BLK, BLK), BLK)
        part = mm(h3[rows, :], x3[:, 0 : ROWS * NZ])
        spec[rows, 0 : ROWS * NZ] = part
        t = 2.0 + (lam_ref[rows, :] + eig)
        u2 = t * t - 1.0
        u3 = t * (t * t - 2.0)
        f = [part[:, r * NZ : (r + 1) * NZ] for r in range(ROWS)]
        first = u3 * f[0] + u2 * f[1] + t * f[2] + f[3]
        second = f[1] + t * f[2] + u2 * f[3] - u3 * spec[rows, ROWS * NZ : (ROWS + 1) * NZ]
        start = pl.multiple_of(z_of[dz] * 512, 512)
        for jj in range(4):
            own = slice(jj * 32, (jj + 1) * 32)
            s2[pl.ds(start + 2 * jj, 32, stride=16), :] = first[own]
            s2[pl.ds(start + 2 * jj + 1, 32, stride=16), :] = second[own]
        send_all(farthest_first([dz]), s2, r2, 16, 9, f_send, f_recv)
    keep_own(s2, r2, 16, 9)

    t = 2.0 + (lam_ref[...] + eig)
    u2 = t * t - 1.0
    u3 = t * (t * t - 2.0)
    w3 = 1.0 / u3
    w1 = u2 * w3
    w2 = t * w3
    f1, f2, f3 = (spec[:, r * NZ : (r + 1) * NZ] for r in range(1, ROWS))
    modal[:, 0:NZ] = w1 * f1 + w2 * f2 + w3 * f3
    modal[:, NZ : 2 * NZ] = w2 * (f1 + t * f2 + f3)
    modal[:, 2 * NZ : 3 * NZ] = w3 * f1 + w2 * f2 + w1 * f3
    wrow[:, 0:NZ] = w1
    wrow[:, NZ : 2 * NZ] = w2
    wrow[:, 2 * NZ : 3 * NZ] = w3

    def store_of(block):
        rows = pl.ds(block * BLK, BLK)
        return pltpu.make_async_copy(outv.at[:, rows], out_hbm.at[:, rows], out_sem.at[block])

    for jj in range(4):
        shift = lam_ref[pl.ds(my_z * 128 + jj * 32 + (me - my_z * 32), 1), :] + eig
        edge = 2.0 + shift
        inv[:, jj * NZ : (jj + 1) * NZ] = 1.0 / (
            edge * edge * shift * (4.0 + shift) + lamx_ref[...]
        )
    for copy in large[6:]:
        copy.wait()
    wait_rows(r2, (RANKS - 1) * 9, f_recv)
    for jj in range(4):
        for h in range(2):
            high, low = split(r2[pl.ds(2 * jj + h, RANKS, stride=16), :])
            for part, value in enumerate((high, low, high)):
                first = part * 2 * RANKS + h * RANKS
                xk[first : first + RANKS, jj * NZ : (jj + 1) * NZ] = value
    solved = mm(hxf_ref[...], xk[...]) * inv[...]
    high, low = split(solved)
    xk[0:RANKS, :] = high
    xk[RANKS : 2 * RANKS, :] = low
    xk[2 * RANKS : 3 * RANKS, :] = high
    both = mm(hxi_ref[...], xk[0 : 3 * RANKS, :])
    for jj in range(4):
        for h in range(2):
            s3[pl.ds(2 * jj + h, RANKS, stride=8), :] = both[
                h * RANKS : (h + 1) * RANKS, jj * NZ : (jj + 1) * NZ
            ]
    for dz in (2, 1, 3, 0):
        send_all(farthest_first([dz]), s3, r3, 8, 8, b_send, b_recv.at[my_z])
    keep_own(s3, r3, 8, 8)

    thinning = lax.dot_general(
        pick, r2[pl.ds(8, RANKS, stride=16), :], contract_first,
        precision=lax.Precision.HIGHEST, preferred_element_type=F32,
    )
    thick_ref[...] = ice_ref[...] - 0.3 * thinning
    synth_high, synth_low = split(synth_ref[...])

    for group, dz in enumerate((2, 3, 1, 0)):
        z = z_of[dz]
        wait_rows(r3, (32 if dz else 31) * 8, b_recv.at[z])
        for jj in range(4):
            first = pl.multiple_of(z * 256, 256) + 2 * jj
            q0 = r3[pl.ds(first, 32, stride=8), :]
            q1 = r3[pl.ds(first + 1, 32, stride=8), :]
            rows = pl.ds(pl.multiple_of(z * BLK, BLK) + jj * 32, 32)
            w1, w2, w3 = (wrow[rows, r * NZ : (r + 1) * NZ] for r in range(3))
            fields = [
                q0,
                w1 * q0 + w3 * q1 + modal[rows, 0:NZ],
                w2 * (q0 + q1) + modal[rows, NZ : 2 * NZ],
                w3 * q0 + w1 * q1 + modal[rows, 2 * NZ : 3 * NZ],
            ]
            for r in range(ROWS):
                high, low = split(fields[r])
                for part, value in enumerate((high, low, high)):
                    start = group * 3 * BLK + part * BLK + jj * 32
                    x3[start : start + 32, r * NZ : (r + 1) * NZ] = value
        right = x3[group * 3 * BLK : (group + 1) * 3 * BLK, 0 : ROWS * NZ]
        if group == 0:
            acc[...] = mm(hb[z], right)
        elif group < NB - 1:
            acc[...] += mm(hb[z], right)
        else:
            for block in range(NB):
                rows = slice(block * BLK, (block + 1) * BLK)
                part = acc[rows, :] + mm(hb[z, rows, :], right)
                for r in range(ROWS):
                    outv[r, rows, :] = mm3(
                        part[:, r * NZ : (r + 1) * NZ], synth_high, synth_low
                    )
                store_of(block).start()

    wait_rows(xs, RANKS - 1, c_send)
    wait_rows(s2, (RANKS - 1) * 9, f_send)
    wait_rows(s3, (RANKS - 1) * 8, b_send)
    for block in range(NB):
        store_of(block).wait()


def hand_over_kernel(
    pressure_hbm, thickness_hbm, out_hbm, thick_hbm, pressure, thickness, in_sem, out_sem
):
    def piece(ref, index):
        return ref.at[index // 2, pl.ds(index % 2 * 256, 256)]

    first = [
        pltpu.make_async_copy(piece(pressure_hbm, i), piece(pressure, i), in_sem.at[i])
        for i in range(8)
    ] + [pltpu.make_async_copy(thickness_hbm, thickness, in_sem.at[8])]
    second = [
        pltpu.make_async_copy(piece(pressure, i), piece(out_hbm, i), out_sem.at[i])
        for i in range(8)
    ] + [pltpu.make_async_copy(thickness, thick_hbm, out_sem.at[8])]
    for copy in first:
        copy.start()
    for copy, following in zip(first, second):
        copy.wait()
        following.start()
    for copy in second:
        copy.wait()


def body(
    velocity,
    layer_depth,
    vertical_modes,
    vertical_synthesis,
    mode_eigen,
    boundary_tracers,
    friction_speed,
    draft_level,
    tile_offset,
    draft_count,
    draft_list,
    exchange_coeff,
    ice_thickness,
):
    hh, hl = split_table(hartley(NY))
    small = hartley(RANKS)
    following = (np.arange(RANKS) + 1) % RANKS
    fwd_high, fwd_low = split_table(np.concatenate([small, small[:, following]], axis=1))
    inv_high, inv_low = split_table(np.concatenate([small, small[following]], axis=0))
    hxf = np.concatenate([fwd_high, fwd_high, fwd_low], axis=1)
    hxi = np.concatenate([inv_high, inv_high, inv_low], axis=1)
    lam = np.repeat(eigen(NY)[:, None], NZ, axis=1).astype(np.float32)
    lamx = np.repeat(eigen(RANKS)[:, None], NZ, axis=1).astype(np.float32)
    vmem = pl.BlockSpec(memory_space=pltpu.VMEM)
    hbm = pl.BlockSpec(memory_space=pltpu.HBM)
    tiles = (RANKS * 8, NZ)
    results = pl.pallas_call(
        kernel,
        out_shape=(
            jax.ShapeDtypeStruct((ROWS, NY, NZ), F32),
            jax.ShapeDtypeStruct((16, 128), F32),
        ),
        in_specs=[hbm] * 19,
        out_specs=(hbm, vmem),
        scratch_shapes=[
            pltpu.VMEM((RANKS, 6 * RANKS), BF16),
            pltpu.VMEM((2 * RANKS, 3 * RANKS), BF16),
            pltpu.VMEM((NY, NZ), F32),
            pltpu.VMEM((RANKS, NZ), F32),
            pltpu.VMEM((1, NZ), F32),
            pltpu.VMEM((NZ, NZ), F32),
            pltpu.VMEM((NZ, NZ), F32),
            pltpu.VMEM((16, 128), F32),
            pltpu.VMEM((1, NZ), F32),
            pltpu.VMEM((2, ROWS, NY), F32),
            pltpu.VMEM((ROWS, NY), F32),
            pltpu.VMEM((ROWS, NY), jnp.int32),
            pltpu.VMEM((1, RANKS), jnp.int32),
            pltpu.VMEM((1, RANKS), jnp.int32),
            pltpu.VMEM((8, RANKS), jnp.int32),
            pltpu.VMEM((16, 128), F32),
            pltpu.VMEM((3, ROWS, NY, NZ), F32),
            pltpu.VMEM((NY, 3 * NY), BF16),
            pltpu.VMEM((3 * NY, (ROWS + 1) * NZ), BF16),
            pltpu.VMEM((NY, ROWS * NZ), F32),
            pltpu.VMEM((NY, (ROWS + 1) * NZ), F32),
            pltpu.VMEM((NY, ROWS * NZ), F32),
            pltpu.VMEM((6 * RANKS, 4 * NZ), BF16),
            pltpu.VMEM((RANKS, 4 * NZ), F32),
            pltpu.VMEM(tiles, F32),
            pltpu.VMEM(tiles, F32),
            pltpu.VMEM((RANKS * 16, NZ), F32),
            pltpu.VMEM((RANKS * 16, NZ), F32),
            pltpu.VMEM(tiles, F32),
            pltpu.VMEM(tiles, F32),
            pltpu.VMEM((NB, NY, 3 * BLK), BF16),
            pltpu.VMEM((NY, ROWS * NZ), F32),
            pltpu.VMEM((ROWS, NY, NZ), F32),
            pltpu.SemaphoreType.DMA((32,)),
            pltpu.SemaphoreType.DMA((NB,)),
            pltpu.SemaphoreType.DMA,
            pltpu.SemaphoreType.DMA,
            pltpu.SemaphoreType.DMA,
            pltpu.SemaphoreType.DMA,
            pltpu.SemaphoreType.DMA,
            pltpu.SemaphoreType.DMA((4,)),
        ],
        compiler_params=pltpu.CompilerParams(
            collective_id=0, has_side_effects=True, vmem_limit_bytes=56 * 2**20
        ),
    )(
        velocity,
        hh,
        hl,
        hxf,
        hxi,
        lam,
        lamx,
        layer_depth.reshape(1, NZ),
        vertical_modes,
        vertical_synthesis,
        ice_thickness.reshape(16, 128),
        mode_eigen.reshape(1, NZ),
        boundary_tracers,
        friction_speed,
        draft_level,
        tile_offset.reshape(1, RANKS),
        draft_count,
        jnp.swapaxes(draft_list, 1, 2).reshape(8, RANKS),
        exchange_coeff.reshape(16, 128),
    )
    pressure, thickness = pl.pallas_call(
        hand_over_kernel,
        out_shape=(
            jax.ShapeDtypeStruct((ROWS, NY, NZ), F32),
            jax.ShapeDtypeStruct((16, 128), F32),
        ),
        in_specs=[hbm] * 2,
        out_specs=(hbm, hbm),
        scratch_shapes=[
            pltpu.VMEM((ROWS, NY, NZ), F32),
            pltpu.VMEM((16, 128), F32),
            pltpu.SemaphoreType.DMA((9,)),
            pltpu.SemaphoreType.DMA((9,)),
        ],
        compiler_params=pltpu.CompilerParams(vmem_limit_bytes=56 * 2**20),
    )(*results)
    return (pressure, thickness.reshape(2048))


def solution(mesh):
    in_specs = (
        P(None, ("px", "py"), None, None),
        P(),
        P(),
        P(),
        P(),
        P(None, ("px", "py"), None),
        P(("px", "py"), None),
        P(("px", "py"), None),
        P(),
        P(("px", "py"), None),
        P(("px", "py"), None, None),
        P(("px", "py")),
        P(("px", "py")),
    )
    out_specs = (P(("px", "py"), None, None), P(("px", "py")))
    return jax.shard_map(body, mesh=mesh, in_specs=in_specs, out_specs=out_specs, check_vma=False)
```

```python
import math
import random

import jax
import jax.numpy as jnp
import numpy as np
from jax import lax
from jax.experimental import pallas as pl
from jax.experimental.pallas import tpu as pltpu
from jax.sharding import PartitionSpec as P

NX = 512
NY = 512
NZ = 128
RANKS = 128
ROWS = 4
NB = 4
BLK = NY // NB
OUT_BLK = 128
MESH = pl.DeviceIdType.MESH
F32 = jnp.float32
BF16 = jnp.bfloat16


def hops(offset):
    dz, dy, dx, dc = offset
    return sum(min(d, 4 - d) for d in (dz, dy, dx))


def farthest_first(dzs):
    offsets = [
        (dz, dy, dx, dc)
        for dz in dzs
        for dy in range(4)
        for dx in range(4)
        for dc in range(2)
        if (dz, dy, dx, dc) != (0, 0, 0, 0)
    ]
    random.Random(2).shuffle(offsets)
    return sorted(offsets, key=lambda offset: -hops(offset))


def hartley(length):
    index = np.arange(length)
    angle = (np.outer(index, index) % length) * (2.0 * math.pi / length)
    return (np.cos(angle) + np.sin(angle)) / math.sqrt(length)


def split_table(table):
    high = np.asarray(table, np.float32).astype(jnp.bfloat16)
    low = (np.asarray(table, np.float32) - high.astype(np.float32)).astype(jnp.bfloat16)
    return high, low


def eigen(length):
    return 2.0 - 2.0 * np.cos(2.0 * math.pi * np.arange(length) / length)


def split(x):
    high = x.astype(BF16)
    return high, (x - high.astype(F32)).astype(BF16)


def mm(a, b):
    return jnp.dot(a, b, preferred_element_type=F32)


def mm_exact_left(a, x):
    high, low = split(x)
    return mm(a, high) + mm(a, low)


def mm_exact_right(x, b):
    high, low = split(x)
    return mm(high, b) + mm(low, b)


def mm3(x, b_high, b_low):
    high, low = split(x)
    return mm(high, b_high) + mm(low, b_high) + mm(high, b_low)


def iota(shape, axis):
    return lax.broadcasted_iota(jnp.int32, shape, axis)


def kernel(
    vel_hbm,
    hh_hbm,
    hl_hbm,
    hxf_hbm,
    hxi_hbm,
    lam_hbm,
    lamx_hbm,
    depth_hbm,
    modes_hbm,
    ice_hbm,
    eig_hbm,
    trac_hbm,
    fric_hbm,
    lvl_hbm,
    off_hbm,
    cnt_hbm,
    list_hbm,
    coeff_hbm,
    out_hbm,
    thick_ref,
    hxf_ref,
    hxi_ref,
    lam_ref,
    lamx_ref,
    depth_ref,
    modes_ref,
    ice_ref,
    eig_ref,
    trac_ref,
    fric_ref,
    lvl_ref,
    off_ref,
    cnt_ref,
    list_ref,
    coeff_ref,
    vel,
    h3,
    x3,
    modal,
    spec,
    wrow,
    xk,
    inv,
    xs,
    xr,
    ms,
    mr,
    s2,
    r2,
    s3,
    r3,
    hb,
    acc,
    load_sem,
    out_sem,
    c_send,
    c_recv,
    m_send,
    m_recv,
    f_send,
    f_recv,
    b_send,
    b_recv,
):
    px = lax.axis_index("px")
    py = lax.axis_index("py")
    my_z, my_c, my_y, my_x = px // 2, px % 2, py // 4, py % 4
    me = px * 16 + py

    def load(source, target, index):
        return pltpu.make_async_copy(source, target, load_sem.at[index])

    small = [
        load(source, target, index)
        for index, (source, target) in enumerate(
            (
                (off_hbm, off_ref),
                (coeff_hbm, coeff_ref),
                (trac_hbm, trac_ref),
                (fric_hbm, fric_ref),
                (lvl_hbm, lvl_ref),
                (cnt_hbm, cnt_ref),
                (list_hbm, list_ref),
                (depth_hbm, depth_ref),
                (modes_hbm, modes_ref),
                (eig_hbm, eig_ref),
            )
        )
    ]
    large = [
        load(source, target, index + len(small))
        for index, (source, target) in enumerate(
            (
                (vel_hbm, vel),
                (hh_hbm, h3.at[:, pl.ds(0, NY)]),
                (hh_hbm, h3.at[:, pl.ds(NY, NY)]),
                (hl_hbm, h3.at[:, pl.ds(2 * NY, NY)]),
                (lam_hbm, lam_ref),
                (lamx_hbm, lamx_ref),
                (hxf_hbm, hxf_ref),
                (hxi_hbm, hxi_ref),
                (ice_hbm, ice_ref),
            )
            + tuple(
                (
                    table.at[:, pl.ds(b * BLK, BLK)],
                    hb.at[b, :, pl.ds(part * BLK, BLK)],
                )
                for b in range(NB)
                for part, table in enumerate((hh_hbm, hh_hbm, hl_hbm))
            )
        )
    ]

    z_of = [(my_z + d) % 4 for d in range(4)]
    c_of = [my_c, 1 - my_c]
    px_of = [[z_of[dz] * 2 + c_of[dc] for dc in range(2)] for dz in range(4)]
    py_of = [[(my_y + dy) % 4 * 4 + (my_x + dx) % 4 for dx in range(4)] for dy in range(4)]
    everyone = farthest_first(range(4))
    barrier = pltpu.get_barrier_semaphore()
    for dz, dy, dx, dc in everyone:
        pl.semaphore_signal(
            barrier, inc=1, device_id=(px_of[dz][dc], py_of[dy][dx]), device_id_type=MESH
        )

    for copy in small + large:
        copy.start()
    for copy in small:
        copy.wait()

    off = off_ref[...]
    sub = iota((RANKS, RANKS), 0)
    lane = iota((RANKS, RANKS), 1)
    tile_row = (iota((RANKS, 16), 0) // 8 == iota((RANKS, 16), 1)).astype(BF16)
    pick = mm(((me - off + RANKS) % RANKS == sub).astype(BF16), tile_row)
    xs[pl.ds(0, RANKS, stride=8), :] = jnp.dot(
        pick, coeff_ref[...], precision=lax.Precision.HIGHEST
    )

    def send_all(offsets, source, target, unit, rows, send_sem, recv_sem):
        for dz, dy, dx, dc in offsets:
            dest_px, dest_py = px_of[dz][dc], py_of[dy][dx]
            first = pl.multiple_of((dest_px * 16 + dest_py) * unit, unit)
            pltpu.make_async_remote_copy(
                src_ref=source.at[pl.ds(first, rows), :],
                dst_ref=target.at[pl.ds(pl.multiple_of(me * unit, unit), rows), :],
                send_sem=send_sem,
                recv_sem=recv_sem,
                device_id=(dest_px, dest_py),
                device_id_type=MESH,
            ).start()

    def keep_own(source, target, unit, rows):
        own = pl.ds(pl.multiple_of(me * unit, unit), rows)
        target[own, :] = source[own, :]

    def wait_rows(ref, rows, sem):
        pltpu.make_async_copy(ref.at[pl.ds(0, rows), :], ref.at[pl.ds(0, rows), :], sem).wait()

    pl.semaphore_wait(barrier, RANKS - 1)
    send_all(everyone, xs, xr, 8, 1, c_send, c_recv)
    keep_own(xs, xr, 8, 1)

    inv_depth = 1.0 / depth_ref[...]
    inv_depth_col = jnp.sum(jnp.where(sub == lane, inv_depth, 0.0), axis=1, keepdims=True)
    level = lvl_ref[...].astype(F32)
    thermal = trac_ref[0] - 0.6 * trac_ref[1] + 1.5 * ((level + 0.5) / NZ) - 0.5
    factor = fric_ref[...] * thermal
    rows_lane = (iota((ROWS, NZ), 1) % 16 // 4 == iota((ROWS, NZ), 0)).astype(F32)
    contract_first = (((0,), (0,)), ((), ()))
    factor_lanes = lax.dot_general(
        factor, rows_lane, contract_first, precision=lax.Precision.HIGHEST,
        preferred_element_type=F32,
    )
    y_sub = iota((NY, NZ), 0)
    y_lane = iota((NY, NZ), 1)
    in_tile = y_sub % 32 == 4 * (y_lane // 16) + y_lane % 4
    tile_of_y = (iota((NY, RANKS), 0) // 4 == iota((NY, RANKS), 1)).astype(BF16)
    tile_from_y = (iota((RANKS, NY), 1) // 4 == iota((RANKS, NY), 0)).astype(BF16)
    by_tile = mm_exact_left(tile_from_y, jnp.where(in_tile, factor_lanes, 0.0))
    cells = jnp.where(iota((8, RANKS), 0) < cnt_ref[...], list_ref[...], -1).astype(F32)
    slot_spread = (iota((8, 8 * NZ), 1) // NZ == iota((8, 8 * NZ), 0)).astype(F32)
    cell_lanes = lax.dot_general(
        cells, slot_spread, contract_first, preferred_element_type=F32
    )
    position = (lane % 16).astype(F32)
    live = cell_lanes[:, 0:NZ] == position
    for slot in range(1, 8):
        live = jnp.logical_or(live, cell_lanes[:, slot * NZ : (slot + 1) * NZ] == position)
    to_owner = ((me + off) % RANKS == sub).astype(BF16)
    factor_owner = mm_exact_left(to_owner, jnp.where(live, by_tile, 0.0))
    owner_of_y = lax.dot_general(
        tile_of_y, to_owner, (((1,), (1,)), ((), ())), preferred_element_type=F32
    ).astype(BF16)

    modes = modes_ref[...]
    mode_high, mode_low = split(modes)
    scaled_high, scaled_low = split(modes * inv_depth_col)
    spread = (iota((ROWS, ROWS * NZ), 1) // NZ == iota((ROWS, ROWS * NZ), 0)).astype(F32)
    level_lanes = lax.dot_general(
        level, spread, contract_first, preferred_element_type=F32
    )
    for r in range(ROWS):
        hot = (level_lanes[:, r * NZ : (r + 1) * NZ] == y_lane.astype(F32)).astype(BF16)
        wrow[:, r * NZ : (r + 1) * NZ] = mm(hot, scaled_high) + mm(hot, scaled_low)
    large[0].wait()

    def put_split(field, r):
        high, low = split(field)
        x3[0:NY, r * NZ : (r + 1) * NZ] = high
        x3[NY : 2 * NY, r * NZ : (r + 1) * NZ] = low
        x3[2 * NY : 3 * NY, r * NZ : (r + 1) * NZ] = high

    def divergence(r):
        east, north, up = vel[0, r], vel[1, r], vel[2, r]
        if r > 0:
            east = east - vel[0, r - 1]
        below = jnp.where(y_lane == 0, 0.0, pltpu.roll(up, 1, axis=1))
        flow = east + (north - pltpu.roll(north, 1, axis=0)) + (up - below) * inv_depth
        modal[:, r * NZ : (r + 1) * NZ] = mm3(flow, mode_high, mode_low)

    for r in range(ROWS):
        divergence(r)
    put_split(mm3(vel[0, ROWS - 1], mode_high, mode_low), ROWS)
    for copy in large[1:6]:
        copy.wait()
    spec[:, ROWS * NZ : (ROWS + 1) * NZ] = mm(h3[...], x3[:, ROWS * NZ : (ROWS + 1) * NZ])
    spread_rows = (
        iota((NZ, ROWS * NZ), 0) % 16 // 4 == iota((NZ, ROWS * NZ), 1) // NZ
    ).astype(BF16)

    wait_rows(xr, RANKS - 1, c_recv)
    melt = xr[pl.ds(0, RANKS, stride=8), :] * factor_owner
    ms[pl.ds(0, RANKS, stride=8), :] = melt
    by_y = jnp.where(in_tile, mm_exact_left(owner_of_y, melt), 0.0)
    melt_lanes = mm_exact_right(by_y, spread_rows)
    for r in range(ROWS):
        cols = slice(r * NZ, (r + 1) * NZ)
        put_split(modal[:, cols] + melt_lanes[:, cols] * wrow[:, cols], r)

    eig = eig_ref[...]

    for dz in (2, 1, 3, 0):
        rows = pl.ds(pl.multiple_of(z_of[dz] * BLK, BLK), BLK)
        part = mm(h3[rows, :], x3[:, 0 : ROWS * NZ])
        spec[rows, 0 : ROWS * NZ] = part
        t = 2.0 + (lam_ref[rows, :] + eig)
        u2 = t * t - 1.0
        u3 = t * (t * t - 2.0)
        f = [part[:, r * NZ : (r + 1) * NZ] for r in range(ROWS)]
        first = u3 * f[0] + u2 * f[1] + t * f[2] + f[3]
        second = f[1] + t * f[2] + u2 * f[3] - u3 * spec[rows, ROWS * NZ : (ROWS + 1) * NZ]
        start = pl.multiple_of(z_of[dz] * 256, 256)
        for jj in range(4):
            own = slice(jj * 32, (jj + 1) * 32)
            s2[pl.ds(start + 2 * jj, 32, stride=8), :] = first[own]
            s2[pl.ds(start + 2 * jj + 1, 32, stride=8), :] = second[own]
        send_all(farthest_first([dz]), s2, r2, 8, 8, f_send, f_recv)
    keep_own(s2, r2, 8, 8)
    send_all(everyone, ms, mr, 8, 1, m_send, m_recv)
    keep_own(ms, mr, 8, 1)

    t = 2.0 + (lam_ref[...] + eig)
    u2 = t * t - 1.0
    u3 = t * (t * t - 2.0)
    w3 = 1.0 / u3
    w1 = u2 * w3
    w2 = t * w3
    f1, f2, f3 = (spec[:, r * NZ : (r + 1) * NZ] for r in range(1, ROWS))
    modal[:, 0:NZ] = w1 * f1 + w2 * f2 + w3 * f3
    modal[:, NZ : 2 * NZ] = w2 * (f1 + t * f2 + f3)
    modal[:, 2 * NZ : 3 * NZ] = w3 * f1 + w2 * f2 + w1 * f3
    wrow[:, 0:NZ] = w1
    wrow[:, NZ : 2 * NZ] = w2
    wrow[:, 2 * NZ : 3 * NZ] = w3

    def store_of(block):
        rows = pl.ds(block * BLK, BLK)
        return pltpu.make_async_copy(acc.at[rows], out_hbm.at[rows], out_sem.at[block])

    for jj in range(4):
        shift = lam_ref[pl.ds(my_z * 128 + jj * 32 + (me - my_z * 32), 1), :] + eig
        edge = 2.0 + shift
        inv[:, jj * NZ : (jj + 1) * NZ] = 1.0 / (
            edge * edge * shift * (4.0 + shift) + lamx_ref[...]
        )
    for copy in large[6:]:
        copy.wait()
    wait_rows(r2, (RANKS - 1) * 8, f_recv)
    for jj in range(4):
        for h in range(2):
            high, low = split(r2[pl.ds(2 * jj + h, RANKS, stride=8), :])
            for part, value in enumerate((high, low, high)):
                first = part * 2 * RANKS + h * RANKS
                xk[first : first + RANKS, jj * NZ : (jj + 1) * NZ] = value
    solved = mm(hxf_ref[...], xk[...]) * inv[...]
    high, low = split(solved)
    xk[0:RANKS, :] = high
    xk[RANKS : 2 * RANKS, :] = low
    xk[2 * RANKS : 3 * RANKS, :] = high
    both = mm(hxi_ref[...], xk[0 : 3 * RANKS, :])
    for jj in range(4):
        for h in range(2):
            s3[pl.ds(2 * jj + h, RANKS, stride=8), :] = both[
                h * RANKS : (h + 1) * RANKS, jj * NZ : (jj + 1) * NZ
            ]
    for dz in (2, 1, 3, 0):
        send_all(farthest_first([dz]), s3, r3, 8, 8, b_send, b_recv.at[my_z])
    keep_own(s3, r3, 8, 8)

    wait_rows(mr, RANKS - 1, m_recv)
    thinning = lax.dot_general(
        pick, mr[pl.ds(0, RANKS, stride=8), :], contract_first,
        precision=lax.Precision.HIGHEST, preferred_element_type=F32,
    )
    thick_ref[...] = ice_ref[...] - 0.3 * thinning

    for group, dz in enumerate((2, 3, 1, 0)):
        z = z_of[dz]
        wait_rows(r3, (32 if dz else 31) * 8, b_recv.at[z])
        for jj in range(4):
            first = pl.multiple_of(z * 256, 256) + 2 * jj
            q0 = r3[pl.ds(first, 32, stride=8), :]
            q1 = r3[pl.ds(first + 1, 32, stride=8), :]
            rows = pl.ds(pl.multiple_of(z * BLK, BLK) + jj * 32, 32)
            w1, w2, w3 = (wrow[rows, r * NZ : (r + 1) * NZ] for r in range(3))
            fields = [
                q0,
                w1 * q0 + w3 * q1 + modal[rows, 0:NZ],
                w2 * (q0 + q1) + modal[rows, NZ : 2 * NZ],
                w3 * q0 + w1 * q1 + modal[rows, 2 * NZ : 3 * NZ],
            ]
            for r in range(ROWS):
                high, low = split(fields[r])
                for part, value in enumerate((high, low, high)):
                    start = group * 3 * BLK + part * BLK + jj * 32
                    x3[start : start + 32, r * NZ : (r + 1) * NZ] = value
        right = x3[group * 3 * BLK : (group + 1) * 3 * BLK, 0 : ROWS * NZ]
        if group == 0:
            acc[...] = mm(hb[z], right)
        elif group < NB - 1:
            acc[...] += mm(hb[z], right)
        else:
            for block in range(NB):
                rows = slice(block * BLK, (block + 1) * BLK)
                acc[rows, :] += mm(hb[z, rows, :], right)
                store_of(block).start()

    wait_rows(xs, RANKS - 1, c_send)
    wait_rows(s2, (RANKS - 1) * 8, f_send)
    wait_rows(ms, RANKS - 1, m_send)
    wait_rows(s3, (RANKS - 1) * 8, b_send)
    for block in range(NB):
        store_of(block).wait()


def synthesis_kernel(
    back_hbm,
    thickness_hbm,
    synth_hbm,
    out_hbm,
    thick_hbm,
    back,
    thickness,
    synth,
    pressure,
    in_sem,
    out_sem,
):
    def rows(index):
        return pl.ds(index * OUT_BLK, OUT_BLK)

    pieces = NY // OUT_BLK
    sources = [(synth_hbm, synth)]
    sources += [(back_hbm.at[rows(i)], back.at[rows(i)]) for i in range(pieces)]
    sources += [(thickness_hbm, thickness)]
    first = [
        pltpu.make_async_copy(source, target, in_sem.at[index])
        for index, (source, target) in enumerate(sources)
    ]
    targets = [(pressure.at[:, rows(i)], out_hbm.at[:, rows(i)]) for i in range(pieces)]
    targets += [(thickness, thick_hbm)]
    second = [
        pltpu.make_async_copy(source, target, out_sem.at[index])
        for index, (source, target) in enumerate(targets)
    ]
    for copy in first:
        copy.start()
    first[0].wait()
    synth_high, synth_low = split(synth[...])
    for i in range(pieces):
        first[1 + i].wait()
        for r in range(ROWS):
            pressure[r, rows(i), :] = mm3(
                back[rows(i), r * NZ : (r + 1) * NZ], synth_high, synth_low
            )
        second[i].start()
    first[1 + pieces].wait()
    second[pieces].start()
    for copy in second:
        copy.wait()


def body(
    velocity,
    layer_depth,
    vertical_modes,
    vertical_synthesis,
    mode_eigen,
    boundary_tracers,
    friction_speed,
    draft_level,
    tile_offset,
    draft_count,
    draft_list,
    exchange_coeff,
    ice_thickness,
):
    hh, hl = split_table(hartley(NY))
    small = hartley(RANKS)
    following = (np.arange(RANKS) + 1) % RANKS
    fwd_high, fwd_low = split_table(np.concatenate([small, small[:, following]], axis=1))
    inv_high, inv_low = split_table(np.concatenate([small, small[following]], axis=0))
    hxf = np.concatenate([fwd_high, fwd_high, fwd_low], axis=1)
    hxi = np.concatenate([inv_high, inv_high, inv_low], axis=1)
    lam = np.repeat(eigen(NY)[:, None], NZ, axis=1).astype(np.float32)
    lamx = np.repeat(eigen(RANKS)[:, None], NZ, axis=1).astype(np.float32)
    vmem = pl.BlockSpec(memory_space=pltpu.VMEM)
    hbm = pl.BlockSpec(memory_space=pltpu.HBM)
    tiles = (RANKS * 8, NZ)
    results = pl.pallas_call(
        kernel,
        out_shape=(
            jax.ShapeDtypeStruct((NY, ROWS * NZ), F32),
            jax.ShapeDtypeStruct((16, 128), F32),
        ),
        in_specs=[hbm] * 18,
        out_specs=(hbm, vmem),
        scratch_shapes=[
            pltpu.VMEM((RANKS, 6 * RANKS), BF16),
            pltpu.VMEM((2 * RANKS, 3 * RANKS), BF16),
            pltpu.VMEM((NY, NZ), F32),
            pltpu.VMEM((RANKS, NZ), F32),
            pltpu.VMEM((1, NZ), F32),
            pltpu.VMEM((NZ, NZ), F32),
            pltpu.VMEM((16, 128), F32),
            pltpu.VMEM((1, NZ), F32),
            pltpu.VMEM((2, ROWS, NY), F32),
            pltpu.VMEM((ROWS, NY), F32),
            pltpu.VMEM((ROWS, NY), jnp.int32),
            pltpu.VMEM((1, RANKS), jnp.int32),
            pltpu.VMEM((1, RANKS), jnp.int32),
            pltpu.VMEM((8, RANKS), jnp.int32),
            pltpu.VMEM((16, 128), F32),
            pltpu.VMEM((3, ROWS, NY, NZ), F32),
            pltpu.VMEM((NY, 3 * NY), BF16),
            pltpu.VMEM((3 * NY, (ROWS + 1) * NZ), BF16),
            pltpu.VMEM((NY, ROWS * NZ), F32),
            pltpu.VMEM((NY, (ROWS + 1) * NZ), F32),
            pltpu.VMEM((NY, ROWS * NZ), F32),
            pltpu.VMEM((6 * RANKS, 4 * NZ), BF16),
            pltpu.VMEM((RANKS, 4 * NZ), F32),
            pltpu.VMEM(tiles, F32),
            pltpu.VMEM(tiles, F32),
            pltpu.VMEM(tiles, F32),
            pltpu.VMEM(tiles, F32),
            pltpu.VMEM(tiles, F32),
            pltpu.VMEM(tiles, F32),
            pltpu.VMEM(tiles, F32),
            pltpu.VMEM(tiles, F32),
            pltpu.VMEM((NB, NY, 3 * BLK), BF16),
            pltpu.VMEM((NY, ROWS * NZ), F32),
            pltpu.SemaphoreType.DMA((31,)),
            pltpu.SemaphoreType.DMA((NB,)),
            pltpu.SemaphoreType.DMA,
            pltpu.SemaphoreType.DMA,
            pltpu.SemaphoreType.DMA,
            pltpu.SemaphoreType.DMA,
            pltpu.SemaphoreType.DMA,
            pltpu.SemaphoreType.DMA,
            pltpu.SemaphoreType.DMA,
            pltpu.SemaphoreType.DMA((4,)),
        ],
        compiler_params=pltpu.CompilerParams(
            collective_id=0, has_side_effects=True, vmem_limit_bytes=56 * 2**20
        ),
    )(
        velocity,
        hh,
        hl,
        hxf,
        hxi,
        lam,
        lamx,
        layer_depth.reshape(1, NZ),
        vertical_modes,
        ice_thickness.reshape(16, 128),
        mode_eigen.reshape(1, NZ),
        boundary_tracers,
        friction_speed,
        draft_level,
        tile_offset.reshape(1, RANKS),
        draft_count,
        jnp.swapaxes(draft_list, 1, 2).reshape(8, RANKS),
        exchange_coeff.reshape(16, 128),
    )
    pressure, thickness = pl.pallas_call(
        synthesis_kernel,
        out_shape=(
            jax.ShapeDtypeStruct((ROWS, NY, NZ), F32),
            jax.ShapeDtypeStruct((16, 128), F32),
        ),
        in_specs=[hbm] * 3,
        out_specs=(hbm, hbm),
        scratch_shapes=[
            pltpu.VMEM((NY, ROWS * NZ), F32),
            pltpu.VMEM((16, 128), F32),
            pltpu.VMEM((NZ, NZ), F32),
            pltpu.VMEM((ROWS, NY, NZ), F32),
            pltpu.SemaphoreType.DMA((NY // OUT_BLK + 2,)),
            pltpu.SemaphoreType.DMA((NY // OUT_BLK + 1,)),
        ],
        compiler_params=pltpu.CompilerParams(vmem_limit_bytes=56 * 2**20),
    )(*results, vertical_synthesis)
    return (pressure, thickness.reshape(2048))


def solution(mesh):
    in_specs = (
        P(None, ("px", "py"), None, None),
        P(),
        P(),
        P(),
        P(),
        P(None, ("px", "py"), None),
        P(("px", "py"), None),
        P(("px", "py"), None),
        P(),
        P(("px", "py"), None),
        P(("px", "py"), None, None),
        P(("px", "py")),
        P(("px", "py")),
    )
    out_specs = (P(("px", "py"), None, None), P(("px", "py")))
    return jax.shard_map(body, mesh=mesh, in_specs=in_specs, out_specs=out_specs, check_vma=False)
```

```python
import math
import random

import jax
import jax.numpy as jnp
import numpy as np
from jax import lax
from jax.experimental import pallas as pl
from jax.experimental.pallas import tpu as pltpu
from jax.sharding import PartitionSpec as P

NX = 512
NY = 512
NZ = 128
RANKS = 128
ROWS = 4
NB = 4
BLK = NY // NB
MESH = pl.DeviceIdType.MESH
F32 = jnp.float32
BF16 = jnp.bfloat16


def hops(offset):
    dz, dy, dx, dc = offset
    return sum(min(d, 4 - d) for d in (dz, dy, dx))


def farthest_first(dzs):
    offsets = [
        (dz, dy, dx, dc)
        for dz in dzs
        for dy in range(4)
        for dx in range(4)
        for dc in range(2)
        if (dz, dy, dx, dc) != (0, 0, 0, 0)
    ]
    random.Random(2).shuffle(offsets)
    return sorted(offsets, key=lambda offset: -hops(offset))


def hartley(length):
    index = np.arange(length)
    angle = (np.outer(index, index) % length) * (2.0 * math.pi / length)
    return (np.cos(angle) + np.sin(angle)) / math.sqrt(length)


def split_table(table):
    high = np.asarray(table, np.float32).astype(jnp.bfloat16)
    low = (np.asarray(table, np.float32) - high.astype(np.float32)).astype(jnp.bfloat16)
    return high, low


def eigen(length):
    return 2.0 - 2.0 * np.cos(2.0 * math.pi * np.arange(length) / length)


def split(x):
    high = x.astype(BF16)
    return high, (x - high.astype(F32)).astype(BF16)


def mm(a, b):
    return jnp.dot(a, b, preferred_element_type=F32)


def mm_exact_left(a, x):
    high, low = split(x)
    return mm(a, high) + mm(a, low)


def mm_exact_right(x, b):
    high, low = split(x)
    return mm(high, b) + mm(low, b)


def mm3(x, b_high, b_low):
    high, low = split(x)
    return mm(high, b_high) + mm(low, b_high) + mm(high, b_low)


def iota(shape, axis):
    return lax.broadcasted_iota(jnp.int32, shape, axis)


def kernel(
    vel_hbm,
    hh_hbm,
    hl_hbm,
    hxf_hbm,
    hxi_hbm,
    lam_hbm,
    lamx_hbm,
    depth_hbm,
    modes_hbm,
    ice_hbm,
    eig_hbm,
    trac_hbm,
    fric_hbm,
    lvl_hbm,
    off_hbm,
    cnt_hbm,
    list_hbm,
    coeff_hbm,
    acc,
    thick_ref,
    hxf_ref,
    hxi_ref,
    lam_ref,
    lamx_ref,
    depth_ref,
    modes_ref,
    ice_ref,
    eig_ref,
    trac_ref,
    fric_ref,
    lvl_ref,
    off_ref,
    cnt_ref,
    list_ref,
    coeff_ref,
    vel,
    h3,
    x3,
    modal,
    spec,
    wrow,
    xk,
    inv,
    xs,
    xr,
    ms,
    mr,
    s2,
    r2,
    s3,
    r3,
    hb,
    load_sem,
    c_send,
    c_recv,
    m_send,
    m_recv,
    f_send,
    f_recv,
    b_send,
    b_recv,
):
    px = lax.axis_index("px")
    py = lax.axis_index("py")
    my_z, my_c, my_y, my_x = px // 2, px % 2, py // 4, py % 4
    me = px * 16 + py

    def load(source, target, index):
        return pltpu.make_async_copy(source, target, load_sem.at[index])

    small = [
        load(source, target, index)
        for index, (source, target) in enumerate(
            (
                (off_hbm, off_ref),
                (coeff_hbm, coeff_ref),
                (trac_hbm, trac_ref),
                (fric_hbm, fric_ref),
                (lvl_hbm, lvl_ref),
                (cnt_hbm, cnt_ref),
                (list_hbm, list_ref),
                (depth_hbm, depth_ref),
                (modes_hbm, modes_ref),
                (eig_hbm, eig_ref),
            )
        )
    ]
    large = [
        load(source, target, index + len(small))
        for index, (source, target) in enumerate(
            (
                (vel_hbm, vel),
                (hh_hbm, h3.at[:, pl.ds(0, NY)]),
                (hh_hbm, h3.at[:, pl.ds(NY, NY)]),
                (hl_hbm, h3.at[:, pl.ds(2 * NY, NY)]),
                (lam_hbm, lam_ref),
                (lamx_hbm, lamx_ref),
                (hxf_hbm, hxf_ref),
                (hxi_hbm, hxi_ref),
                (ice_hbm, ice_ref),
            )
            + tuple(
                (
                    table.at[:, pl.ds(b * BLK, BLK)],
                    hb.at[b, :, pl.ds(part * BLK, BLK)],
                )
                for b in range(NB)
                for part, table in enumerate((hh_hbm, hh_hbm, hl_hbm))
            )
        )
    ]

    z_of = [(my_z + d) % 4 for d in range(4)]
    c_of = [my_c, 1 - my_c]
    px_of = [[z_of[dz] * 2 + c_of[dc] for dc in range(2)] for dz in range(4)]
    py_of = [[(my_y + dy) % 4 * 4 + (my_x + dx) % 4 for dx in range(4)] for dy in range(4)]
    everyone = farthest_first(range(4))
    barrier = pltpu.get_barrier_semaphore()
    for dz, dy, dx, dc in everyone:
        pl.semaphore_signal(
            barrier, inc=1, device_id=(px_of[dz][dc], py_of[dy][dx]), device_id_type=MESH
        )

    for copy in small + large:
        copy.start()
    for copy in small:
        copy.wait()

    off = off_ref[...]
    sub = iota((RANKS, RANKS), 0)
    lane = iota((RANKS, RANKS), 1)
    tile_row = (iota((RANKS, 16), 0) // 8 == iota((RANKS, 16), 1)).astype(BF16)
    pick = mm(((me - off + RANKS) % RANKS == sub).astype(BF16), tile_row)
    xs[pl.ds(0, RANKS, stride=8), :] = jnp.dot(
        pick, coeff_ref[...], precision=lax.Precision.HIGHEST
    )

    def send_all(offsets, source, target, unit, rows, send_sem, recv_sem):
        for dz, dy, dx, dc in offsets:
            dest_px, dest_py = px_of[dz][dc], py_of[dy][dx]
            first = pl.multiple_of((dest_px * 16 + dest_py) * unit, unit)
            pltpu.make_async_remote_copy(
                src_ref=source.at[pl.ds(first, rows), :],
                dst_ref=target.at[pl.ds(pl.multiple_of(me * unit, unit), rows), :],
                send_sem=send_sem,
                recv_sem=recv_sem,
                device_id=(dest_px, dest_py),
                device_id_type=MESH,
            ).start()

    def keep_own(source, target, unit, rows):
        own = pl.ds(pl.multiple_of(me * unit, unit), rows)
        target[own, :] = source[own, :]

    def wait_rows(ref, rows, sem):
        pltpu.make_async_copy(ref.at[pl.ds(0, rows), :], ref.at[pl.ds(0, rows), :], sem).wait()

    pl.semaphore_wait(barrier, RANKS - 1)
    send_all(everyone, xs, xr, 8, 1, c_send, c_recv)
    keep_own(xs, xr, 8, 1)

    inv_depth = 1.0 / depth_ref[...]
    inv_depth_col = jnp.sum(jnp.where(sub == lane, inv_depth, 0.0), axis=1, keepdims=True)
    level = lvl_ref[...].astype(F32)
    thermal = trac_ref[0] - 0.6 * trac_ref[1] + 1.5 * ((level + 0.5) / NZ) - 0.5
    factor = fric_ref[...] * thermal
    rows_lane = (iota((ROWS, NZ), 1) % 16 // 4 == iota((ROWS, NZ), 0)).astype(F32)
    contract_first = (((0,), (0,)), ((), ()))
    factor_lanes = lax.dot_general(
        factor, rows_lane, contract_first, precision=lax.Precision.HIGHEST,
        preferred_element_type=F32,
    )
    y_sub = iota((NY, NZ), 0)
    y_lane = iota((NY, NZ), 1)
    in_tile = y_sub % 32 == 4 * (y_lane // 16) + y_lane % 4
    tile_of_y = (iota((NY, RANKS), 0) // 4 == iota((NY, RANKS), 1)).astype(BF16)
    tile_from_y = (iota((RANKS, NY), 1) // 4 == iota((RANKS, NY), 0)).astype(BF16)
    by_tile = mm_exact_left(tile_from_y, jnp.where(in_tile, factor_lanes, 0.0))
    cells = jnp.where(iota((8, RANKS), 0) < cnt_ref[...], list_ref[...], -1).astype(F32)
    slot_spread = (iota((8, 8 * NZ), 1) // NZ == iota((8, 8 * NZ), 0)).astype(F32)
    cell_lanes = lax.dot_general(
        cells, slot_spread, contract_first, preferred_element_type=F32
    )
    position = (lane % 16).astype(F32)
    live = cell_lanes[:, 0:NZ] == position
    for slot in range(1, 8):
        live = jnp.logical_or(live, cell_lanes[:, slot * NZ : (slot + 1) * NZ] == position)
    to_owner = ((me + off) % RANKS == sub).astype(BF16)
    factor_owner = mm_exact_left(to_owner, jnp.where(live, by_tile, 0.0))
    owner_of_y = lax.dot_general(
        tile_of_y, to_owner, (((1,), (1,)), ((), ())), preferred_element_type=F32
    ).astype(BF16)

    modes = modes_ref[...]
    mode_high, mode_low = split(modes)
    scaled_high, scaled_low = split(modes * inv_depth_col)
    spread = (iota((ROWS, ROWS * NZ), 1) // NZ == iota((ROWS, ROWS * NZ), 0)).astype(F32)
    level_lanes = lax.dot_general(
        level, spread, contract_first, preferred_element_type=F32
    )
    for r in range(ROWS):
        hot = (level_lanes[:, r * NZ : (r + 1) * NZ] == y_lane.astype(F32)).astype(BF16)
        wrow[:, r * NZ : (r + 1) * NZ] = mm(hot, scaled_high) + mm(hot, scaled_low)
    large[0].wait()

    def put_split(field, r):
        high, low = split(field)
        x3[0:NY, r * NZ : (r + 1) * NZ] = high
        x3[NY : 2 * NY, r * NZ : (r + 1) * NZ] = low
        x3[2 * NY : 3 * NY, r * NZ : (r + 1) * NZ] = high

    def divergence(r):
        east, north, up = vel[0, r], vel[1, r], vel[2, r]
        if r > 0:
            east = east - vel[0, r - 1]
        below = jnp.where(y_lane == 0, 0.0, pltpu.roll(up, 1, axis=1))
        flow = east + (north - pltpu.roll(north, 1, axis=0)) + (up - below) * inv_depth
        modal[:, r * NZ : (r + 1) * NZ] = mm3(flow, mode_high, mode_low)

    for r in range(ROWS):
        divergence(r)
    put_split(mm3(vel[0, ROWS - 1], mode_high, mode_low), ROWS)
    for copy in large[1:6]:
        copy.wait()
    spec[:, ROWS * NZ : (ROWS + 1) * NZ] = mm(h3[...], x3[:, ROWS * NZ : (ROWS + 1) * NZ])
    spread_rows = (
        iota((NZ, ROWS * NZ), 0) % 16 // 4 == iota((NZ, ROWS * NZ), 1) // NZ
    ).astype(BF16)

    wait_rows(xr, RANKS - 1, c_recv)
    melt = xr[pl.ds(0, RANKS, stride=8), :] * factor_owner
    ms[pl.ds(0, RANKS, stride=8), :] = melt
    by_y = jnp.where(in_tile, mm_exact_left(owner_of_y, melt), 0.0)
    melt_lanes = mm_exact_right(by_y, spread_rows)
    for r in range(ROWS):
        cols = slice(r * NZ, (r + 1) * NZ)
        put_split(modal[:, cols] + melt_lanes[:, cols] * wrow[:, cols], r)

    eig = eig_ref[...]

    for dz in (2, 1, 3, 0):
        rows = pl.ds(pl.multiple_of(z_of[dz] * BLK, BLK), BLK)
        part = mm(h3[rows, :], x3[:, 0 : ROWS * NZ])
        spec[rows, 0 : ROWS * NZ] = part
        t = 2.0 + (lam_ref[rows, :] + eig)
        u2 = t * t - 1.0
        u3 = t * (t * t - 2.0)
        f = [part[:, r * NZ : (r + 1) * NZ] for r in range(ROWS)]
        first = u3 * f[0] + u2 * f[1] + t * f[2] + f[3]
        second = f[1] + t * f[2] + u2 * f[3] - u3 * spec[rows, ROWS * NZ : (ROWS + 1) * NZ]
        start = pl.multiple_of(z_of[dz] * 256, 256)
        for jj in range(4):
            own = slice(jj * 32, (jj + 1) * 32)
            s2[pl.ds(start + 2 * jj, 32, stride=8), :] = first[own]
            s2[pl.ds(start + 2 * jj + 1, 32, stride=8), :] = second[own]
        send_all(farthest_first([dz]), s2, r2, 8, 8, f_send, f_recv)
    keep_own(s2, r2, 8, 8)
    send_all(everyone, ms, mr, 8, 1, m_send, m_recv)
    keep_own(ms, mr, 8, 1)

    t = 2.0 + (lam_ref[...] + eig)
    u2 = t * t - 1.0
    u3 = t * (t * t - 2.0)
    w3 = 1.0 / u3
    w1 = u2 * w3
    w2 = t * w3
    f1, f2, f3 = (spec[:, r * NZ : (r + 1) * NZ] for r in range(1, ROWS))
    modal[:, 0:NZ] = w1 * f1 + w2 * f2 + w3 * f3
    modal[:, NZ : 2 * NZ] = w2 * (f1 + t * f2 + f3)
    modal[:, 2 * NZ : 3 * NZ] = w3 * f1 + w2 * f2 + w1 * f3
    wrow[:, 0:NZ] = w1
    wrow[:, NZ : 2 * NZ] = w2
    wrow[:, 2 * NZ : 3 * NZ] = w3

    for jj in range(4):
        shift = lam_ref[pl.ds(my_z * 128 + jj * 32 + (me - my_z * 32), 1), :] + eig
        edge = 2.0 + shift
        inv[:, jj * NZ : (jj + 1) * NZ] = 1.0 / (
            edge * edge * shift * (4.0 + shift) + lamx_ref[...]
        )
    for copy in large[6:]:
        copy.wait()
    wait_rows(r2, (RANKS - 1) * 8, f_recv)
    for jj in range(4):
        for h in range(2):
            high, low = split(r2[pl.ds(2 * jj + h, RANKS, stride=8), :])
            for part, value in enumerate((high, low, high)):
                first = part * 2 * RANKS + h * RANKS
                xk[first : first + RANKS, jj * NZ : (jj + 1) * NZ] = value
    solved = mm(hxf_ref[...], xk[...]) * inv[...]
    high, low = split(solved)
    xk[0:RANKS, :] = high
    xk[RANKS : 2 * RANKS, :] = low
    xk[2 * RANKS : 3 * RANKS, :] = high
    both = mm(hxi_ref[...], xk[0 : 3 * RANKS, :])
    for jj in range(4):
        for h in range(2):
            s3[pl.ds(2 * jj + h, RANKS, stride=8), :] = both[
                h * RANKS : (h + 1) * RANKS, jj * NZ : (jj + 1) * NZ
            ]
    for dz in (2, 1, 3, 0):
        send_all(farthest_first([dz]), s3, r3, 8, 8, b_send, b_recv.at[my_z])
    keep_own(s3, r3, 8, 8)

    wait_rows(mr, RANKS - 1, m_recv)
    thinning = lax.dot_general(
        pick, mr[pl.ds(0, RANKS, stride=8), :], contract_first,
        precision=lax.Precision.HIGHEST, preferred_element_type=F32,
    )
    thick_ref[...] = ice_ref[...] - 0.3 * thinning

    for group, dz in enumerate((2, 3, 1, 0)):
        z = z_of[dz]
        wait_rows(r3, (32 if dz else 31) * 8, b_recv.at[z])
        for jj in range(4):
            first = pl.multiple_of(z * 256, 256) + 2 * jj
            q0 = r3[pl.ds(first, 32, stride=8), :]
            q1 = r3[pl.ds(first + 1, 32, stride=8), :]
            rows = pl.ds(pl.multiple_of(z * BLK, BLK) + jj * 32, 32)
            w1, w2, w3 = (wrow[rows, r * NZ : (r + 1) * NZ] for r in range(3))
            fields = [
                q0,
                w1 * q0 + w3 * q1 + modal[rows, 0:NZ],
                w2 * (q0 + q1) + modal[rows, NZ : 2 * NZ],
                w3 * q0 + w1 * q1 + modal[rows, 2 * NZ : 3 * NZ],
            ]
            for r in range(ROWS):
                high, low = split(fields[r])
                for part, value in enumerate((high, low, high)):
                    start = group * 3 * BLK + part * BLK + jj * 32
                    x3[start : start + 32, r * NZ : (r + 1) * NZ] = value
        right = x3[group * 3 * BLK : (group + 1) * 3 * BLK, 0 : ROWS * NZ]
        if group == 0:
            acc[...] = mm(hb[z], right)
        elif group < NB - 1:
            acc[...] += mm(hb[z], right)
        else:
            for block in range(NB):
                rows = slice(block * BLK, (block + 1) * BLK)
                acc[rows, :] += mm(hb[z, rows, :], right)

    wait_rows(xs, RANKS - 1, c_send)
    wait_rows(s2, (RANKS - 1) * 8, f_send)
    wait_rows(ms, RANKS - 1, m_send)
    wait_rows(s3, (RANKS - 1) * 8, b_send)


def synthesis_kernel(back, thickness, synth, out_hbm, thick_hbm, pressure, sem):
    thick = pltpu.make_async_copy(thickness, thick_hbm, sem.at[NB])
    thick.start()
    synth_high, synth_low = split(synth[...])
    stores = []
    for i in range(NB):
        rows = pl.ds(i * BLK, BLK)
        for r in range(ROWS):
            pressure[r, rows, :] = mm3(
                back[rows, r * NZ : (r + 1) * NZ], synth_high, synth_low
            )
        stores.append(
            pltpu.make_async_copy(pressure.at[:, rows], out_hbm.at[:, rows], sem.at[i])
        )
        stores[-1].start()
    for copy in stores + [thick]:
        copy.wait()


def body(
    velocity,
    layer_depth,
    vertical_modes,
    vertical_synthesis,
    mode_eigen,
    boundary_tracers,
    friction_speed,
    draft_level,
    tile_offset,
    draft_count,
    draft_list,
    exchange_coeff,
    ice_thickness,
):
    hh, hl = split_table(hartley(NY))
    small = hartley(RANKS)
    following = (np.arange(RANKS) + 1) % RANKS
    fwd_high, fwd_low = split_table(np.concatenate([small, small[:, following]], axis=1))
    inv_high, inv_low = split_table(np.concatenate([small, small[following]], axis=0))
    hxf = np.concatenate([fwd_high, fwd_high, fwd_low], axis=1)
    hxi = np.concatenate([inv_high, inv_high, inv_low], axis=1)
    lam = np.repeat(eigen(NY)[:, None], NZ, axis=1).astype(np.float32)
    lamx = np.repeat(eigen(RANKS)[:, None], NZ, axis=1).astype(np.float32)
    vmem = pl.BlockSpec(memory_space=pltpu.VMEM)
    hbm = pl.BlockSpec(memory_space=pltpu.HBM)
    tiles = (RANKS * 8, NZ)
    results = pl.pallas_call(
        kernel,
        out_shape=(
            jax.ShapeDtypeStruct((NY, ROWS * NZ), F32),
            jax.ShapeDtypeStruct((16, 128), F32),
        ),
        in_specs=[hbm] * 18,
        out_specs=(vmem, vmem),
        scratch_shapes=[
            pltpu.VMEM((RANKS, 6 * RANKS), BF16),
            pltpu.VMEM((2 * RANKS, 3 * RANKS), BF16),
            pltpu.VMEM((NY, NZ), F32),
            pltpu.VMEM((RANKS, NZ), F32),
            pltpu.VMEM((1, NZ), F32),
            pltpu.VMEM((NZ, NZ), F32),
            pltpu.VMEM((16, 128), F32),
            pltpu.VMEM((1, NZ), F32),
            pltpu.VMEM((2, ROWS, NY), F32),
            pltpu.VMEM((ROWS, NY), F32),
            pltpu.VMEM((ROWS, NY), jnp.int32),
            pltpu.VMEM((1, RANKS), jnp.int32),
            pltpu.VMEM((1, RANKS), jnp.int32),
            pltpu.VMEM((8, RANKS), jnp.int32),
            pltpu.VMEM((16, 128), F32),
            pltpu.VMEM((3, ROWS, NY, NZ), F32),
            pltpu.VMEM((NY, 3 * NY), BF16),
            pltpu.VMEM((3 * NY, (ROWS + 1) * NZ), BF16),
            pltpu.VMEM((NY, ROWS * NZ), F32),
            pltpu.VMEM((NY, (ROWS + 1) * NZ), F32),
            pltpu.VMEM((NY, ROWS * NZ), F32),
            pltpu.VMEM((6 * RANKS, 4 * NZ), BF16),
            pltpu.VMEM((RANKS, 4 * NZ), F32),
            pltpu.VMEM(tiles, F32),
            pltpu.VMEM(tiles, F32),
            pltpu.VMEM(tiles, F32),
            pltpu.VMEM(tiles, F32),
            pltpu.VMEM(tiles, F32),
            pltpu.VMEM(tiles, F32),
            pltpu.VMEM(tiles, F32),
            pltpu.VMEM(tiles, F32),
            pltpu.VMEM((NB, NY, 3 * BLK), BF16),
            pltpu.SemaphoreType.DMA((31,)),
            pltpu.SemaphoreType.DMA,
            pltpu.SemaphoreType.DMA,
            pltpu.SemaphoreType.DMA,
            pltpu.SemaphoreType.DMA,
            pltpu.SemaphoreType.DMA,
            pltpu.SemaphoreType.DMA,
            pltpu.SemaphoreType.DMA,
            pltpu.SemaphoreType.DMA((4,)),
        ],
        compiler_params=pltpu.CompilerParams(
            collective_id=0, has_side_effects=True, vmem_limit_bytes=32 * 2**20
        ),
    )(*(pltpu.with_memory_space_constraint(jnp.asarray(x), pltpu.HBM) for x in (
        velocity,
        hh,
        hl,
        hxf,
        hxi,
        lam,
        lamx,
        layer_depth.reshape(1, NZ),
        vertical_modes,
        ice_thickness.reshape(16, 128),
        mode_eigen.reshape(1, NZ),
        boundary_tracers,
        friction_speed,
        draft_level,
        tile_offset.reshape(1, RANKS),
        draft_count,
        jnp.swapaxes(draft_list, 1, 2).reshape(8, RANKS),
        exchange_coeff.reshape(16, 128),
    )))
    pressure, thickness = pl.pallas_call(
        synthesis_kernel,
        out_shape=(
            jax.ShapeDtypeStruct((ROWS, NY, NZ), F32),
            jax.ShapeDtypeStruct((16, 128), F32),
        ),
        in_specs=[vmem] * 3,
        out_specs=(hbm, hbm),
        scratch_shapes=[
            pltpu.VMEM((ROWS, NY, NZ), F32),
            pltpu.SemaphoreType.DMA((NB + 1,)),
        ],
        compiler_params=pltpu.CompilerParams(vmem_limit_bytes=16 * 2**20),
    )(*results, vertical_synthesis)
    return (pressure, thickness.reshape(2048))


def solution(mesh):
    in_specs = (
        P(None, ("px", "py"), None, None),
        P(),
        P(),
        P(),
        P(),
        P(None, ("px", "py"), None),
        P(("px", "py"), None),
        P(("px", "py"), None),
        P(),
        P(("px", "py"), None),
        P(("px", "py"), None, None),
        P(("px", "py")),
        P(("px", "py")),
    )
    out_specs = (P(("px", "py"), None, None), P(("px", "py")))
    return jax.shard_map(body, mesh=mesh, in_specs=in_specs, out_specs=out_specs, check_vma=False)
```

```python
import math
import random

import jax
import jax.numpy as jnp
import numpy as np
from jax import lax
from jax.experimental import pallas as pl
from jax.experimental.pallas import tpu as pltpu
from jax.sharding import PartitionSpec as P

NX = 512
NY = 512
NZ = 128
RANKS = 128
ROWS = 4
NB = 4
BLK = NY // NB
MESH = pl.DeviceIdType.MESH
F32 = jnp.float32
BF16 = jnp.bfloat16


def hops(offset):
    dz, dy, dx, dc = offset
    return sum(min(d, 4 - d) for d in (dz, dy, dx))


def farthest_first(dzs):
    offsets = [
        (dz, dy, dx, dc)
        for dz in dzs
        for dy in range(4)
        for dx in range(4)
        for dc in range(2)
        if (dz, dy, dx, dc) != (0, 0, 0, 0)
    ]
    random.Random(2).shuffle(offsets)
    return sorted(offsets, key=lambda offset: -hops(offset))


def hartley(length):
    index = np.arange(length)
    angle = (np.outer(index, index) % length) * (2.0 * math.pi / length)
    return (np.cos(angle) + np.sin(angle)) / math.sqrt(length)


def split_table(table):
    high = np.asarray(table, np.float32).astype(jnp.bfloat16)
    low = (np.asarray(table, np.float32) - high.astype(np.float32)).astype(jnp.bfloat16)
    return high, low


def eigen(length):
    return 2.0 - 2.0 * np.cos(2.0 * math.pi * np.arange(length) / length)


def split(x):
    high = x.astype(BF16)
    return high, (x - high.astype(F32)).astype(BF16)


def mm(a, b):
    return jnp.dot(a, b, preferred_element_type=F32)


def mm_exact_left(a, x):
    high, low = split(x)
    return mm(a, high) + mm(a, low)


def mm_exact_right(x, b):
    high, low = split(x)
    return mm(high, b) + mm(low, b)


def mm3(x, b_high, b_low):
    high, low = split(x)
    return mm(high, b_high) + mm(low, b_high) + mm(high, b_low)


def iota(shape, axis):
    return lax.broadcasted_iota(jnp.int32, shape, axis)


def kernel(
    vel_hbm,
    hh_hbm,
    hl_hbm,
    hxf_hbm,
    hxi_hbm,
    lam_hbm,
    lamx_hbm,
    depth_hbm,
    modes_hbm,
    ice_hbm,
    eig_hbm,
    trac_hbm,
    fric_hbm,
    lvl_hbm,
    off_hbm,
    cnt_hbm,
    list_hbm,
    coeff_hbm,
    acc,
    thick_ref,
    hxf_ref,
    hxi_ref,
    lam_ref,
    lamx_ref,
    depth_ref,
    modes_ref,
    ice_ref,
    eig_ref,
    trac_ref,
    fric_ref,
    lvl_ref,
    off_ref,
    cnt_ref,
    list_ref,
    coeff_ref,
    vel,
    h3,
    x3,
    modal,
    spec,
    wrow,
    xk,
    inv,
    xs,
    xr,
    ms,
    mr,
    s2,
    r2,
    s3,
    r3,
    hb,
    load_sem,
    c_send,
    c_recv,
    m_send,
    m_recv,
    f_send,
    f_recv,
    b_send,
    b_recv,
):
    px = lax.axis_index("px")
    py = lax.axis_index("py")
    my_z, my_c, my_y, my_x = px // 2, px % 2, py // 4, py % 4
    me = px * 16 + py

    def load(source, target, index):
        return pltpu.make_async_copy(source, target, load_sem.at[index])

    small = [
        load(source, target, index)
        for index, (source, target) in enumerate(
            (
                (off_hbm, off_ref),
                (coeff_hbm, coeff_ref),
                (trac_hbm, trac_ref),
                (fric_hbm, fric_ref),
                (lvl_hbm, lvl_ref),
                (cnt_hbm, cnt_ref),
                (list_hbm, list_ref),
                (depth_hbm, depth_ref),
                (modes_hbm, modes_ref),
                (eig_hbm, eig_ref),
            )
        )
    ]
    large = [
        load(source, target, index + len(small))
        for index, (source, target) in enumerate(
            (
                (vel_hbm, vel),
                (hh_hbm, h3.at[:, pl.ds(0, NY)]),
                (hh_hbm, h3.at[:, pl.ds(NY, NY)]),
                (hl_hbm, h3.at[:, pl.ds(2 * NY, NY)]),
                (lam_hbm, lam_ref),
                (lamx_hbm, lamx_ref),
                (hxf_hbm, hxf_ref),
                (hxi_hbm, hxi_ref),
                (ice_hbm, ice_ref),
            )
            + tuple(
                (
                    table.at[:, pl.ds(b * BLK, BLK)],
                    hb.at[b, :, pl.ds(part * BLK, BLK)],
                )
                for b in range(NB)
                for part, table in enumerate((hh_hbm, hh_hbm, hl_hbm))
            )
        )
    ]

    z_of = [(my_z + d) % 4 for d in range(4)]
    c_of = [my_c, 1 - my_c]
    px_of = [[z_of[dz] * 2 + c_of[dc] for dc in range(2)] for dz in range(4)]
    py_of = [[(my_y + dy) % 4 * 4 + (my_x + dx) % 4 for dx in range(4)] for dy in range(4)]
    everyone = farthest_first(range(4))
    barrier = pltpu.get_barrier_semaphore()
    for dz, dy, dx, dc in everyone:
        pl.semaphore_signal(
            barrier, inc=1, device_id=(px_of[dz][dc], py_of[dy][dx]), device_id_type=MESH
        )

    for copy in small + large:
        copy.start()
    for copy in small:
        copy.wait()

    off = off_ref[...]
    sub = iota((RANKS, RANKS), 0)
    lane = iota((RANKS, RANKS), 1)
    tile_row = (iota((RANKS, 16), 0) // 8 == iota((RANKS, 16), 1)).astype(BF16)
    pick = mm(((me - off + RANKS) % RANKS == sub).astype(BF16), tile_row)
    xs[pl.ds(0, RANKS, stride=8), :] = jnp.dot(
        pick, coeff_ref[...], precision=lax.Precision.HIGHEST
    )

    def send_all(offsets, source, target, unit, rows, send_sem, recv_sem):
        for dz, dy, dx, dc in offsets:
            dest_px, dest_py = px_of[dz][dc], py_of[dy][dx]
            first = pl.multiple_of((dest_px * 16 + dest_py) * unit, unit)
            pltpu.make_async_remote_copy(
                src_ref=source.at[pl.ds(first, rows), :],
                dst_ref=target.at[pl.ds(pl.multiple_of(me * unit, unit), rows), :],
                send_sem=send_sem,
                recv_sem=recv_sem,
                device_id=(dest_px, dest_py),
                device_id_type=MESH,
            ).start()

    def keep_own(source, target, unit, rows):
        own = pl.ds(pl.multiple_of(me * unit, unit), rows)
        target[own, :] = source[own, :]

    def wait_rows(ref, rows, sem):
        pltpu.make_async_copy(ref.at[pl.ds(0, rows), :], ref.at[pl.ds(0, rows), :], sem).wait()

    pl.semaphore_wait(barrier, RANKS - 1)
    send_all(everyone, xs, xr, 8, 1, c_send, c_recv)
    keep_own(xs, xr, 8, 1)

    inv_depth = 1.0 / depth_ref[...]
    inv_depth_col = jnp.sum(jnp.where(sub == lane, inv_depth, 0.0), axis=1, keepdims=True)
    level = lvl_ref[...].astype(F32)
    thermal = trac_ref[0] - 0.6 * trac_ref[1] + 1.5 * ((level + 0.5) / NZ) - 0.5
    factor = fric_ref[...] * thermal
    rows_lane = (iota((ROWS, NZ), 1) % 16 // 4 == iota((ROWS, NZ), 0)).astype(F32)
    contract_first = (((0,), (0,)), ((), ()))
    factor_lanes = lax.dot_general(
        factor, rows_lane, contract_first, precision=lax.Precision.HIGHEST,
        preferred_element_type=F32,
    )
    y_sub = iota((NY, NZ), 0)
    y_lane = iota((NY, NZ), 1)
    in_tile = y_sub % 32 == 4 * (y_lane // 16) + y_lane % 4
    tile_of_y = (iota((NY, RANKS), 0) // 4 == iota((NY, RANKS), 1)).astype(BF16)
    tile_from_y = (iota((RANKS, NY), 1) // 4 == iota((RANKS, NY), 0)).astype(BF16)
    by_tile = mm_exact_left(tile_from_y, jnp.where(in_tile, factor_lanes, 0.0))
    cells = jnp.where(iota((8, RANKS), 0) < cnt_ref[...], list_ref[...], -1).astype(F32)
    slot_spread = (iota((8, 8 * NZ), 1) // NZ == iota((8, 8 * NZ), 0)).astype(F32)
    cell_lanes = lax.dot_general(
        cells, slot_spread, contract_first, preferred_element_type=F32
    )
    position = (lane % 16).astype(F32)
    live = cell_lanes[:, 0:NZ] == position
    for slot in range(1, 8):
        live = jnp.logical_or(live, cell_lanes[:, slot * NZ : (slot + 1) * NZ] == position)
    to_owner = ((me + off) % RANKS == sub).astype(BF16)
    factor_owner = mm_exact_left(to_owner, jnp.where(live, by_tile, 0.0))
    owner_of_y = lax.dot_general(
        tile_of_y, to_owner, (((1,), (1,)), ((), ())), preferred_element_type=F32
    ).astype(BF16)

    modes = modes_ref[...]
    mode_high, mode_low = split(modes)
    scaled_high, scaled_low = split(modes * inv_depth_col)
    spread = (iota((ROWS, ROWS * NZ), 1) // NZ == iota((ROWS, ROWS * NZ), 0)).astype(F32)
    level_lanes = lax.dot_general(
        level, spread, contract_first, preferred_element_type=F32
    )
    for r in range(ROWS):
        hot = (level_lanes[:, r * NZ : (r + 1) * NZ] == y_lane.astype(F32)).astype(BF16)
        wrow[:, r * NZ : (r + 1) * NZ] = mm(hot, scaled_high) + mm(hot, scaled_low)
    large[0].wait()

    def put_split(field, r):
        high, low = split(field)
        x3[0:NY, r * NZ : (r + 1) * NZ] = high
        x3[NY : 2 * NY, r * NZ : (r + 1) * NZ] = low
        x3[2 * NY : 3 * NY, r * NZ : (r + 1) * NZ] = high

    def divergence(r):
        east, north, up = vel[0, r], vel[1, r], vel[2, r]
        if r > 0:
            east = east - vel[0, r - 1]
        below = jnp.where(y_lane == 0, 0.0, pltpu.roll(up, 1, axis=1))
        flow = east + (north - pltpu.roll(north, 1, axis=0)) + (up - below) * inv_depth
        modal[:, r * NZ : (r + 1) * NZ] = mm3(flow, mode_high, mode_low)

    for r in range(ROWS):
        divergence(r)
    put_split(mm3(vel[0, ROWS - 1], mode_high, mode_low), ROWS)
    for copy in large[1:6]:
        copy.wait()
    spec[:, ROWS * NZ : (ROWS + 1) * NZ] = mm(h3[...], x3[:, ROWS * NZ : (ROWS + 1) * NZ])
    spread_rows = (
        iota((NZ, ROWS * NZ), 0) % 16 // 4 == iota((NZ, ROWS * NZ), 1) // NZ
    ).astype(BF16)

    wait_rows(xr, RANKS - 1, c_recv)
    melt = xr[pl.ds(0, RANKS, stride=8), :] * factor_owner
    ms[pl.ds(0, RANKS, stride=8), :] = melt
    by_y = jnp.where(in_tile, mm_exact_left(owner_of_y, melt), 0.0)
    melt_lanes = mm_exact_right(by_y, spread_rows)
    for r in range(ROWS):
        cols = slice(r * NZ, (r + 1) * NZ)
        put_split(modal[:, cols] + melt_lanes[:, cols] * wrow[:, cols], r)

    eig = eig_ref[...]

    for dz in (2, 1, 3, 0):
        rows = pl.ds(pl.multiple_of(z_of[dz] * BLK, BLK), BLK)
        part = mm(h3[rows, :], x3[:, 0 : ROWS * NZ])
        spec[rows, 0 : ROWS * NZ] = part
        t = 2.0 + (lam_ref[rows, :] + eig)
        u2 = t * t - 1.0
        u3 = t * (t * t - 2.0)
        f = [part[:, r * NZ : (r + 1) * NZ] for r in range(ROWS)]
        first = u3 * f[0] + u2 * f[1] + t * f[2] + f[3]
        second = f[1] + t * f[2] + u2 * f[3] - u3 * spec[rows, ROWS * NZ : (ROWS + 1) * NZ]
        start = pl.multiple_of(z_of[dz] * 256, 256)
        for jj in range(4):
            own = slice(jj * 32, (jj + 1) * 32)
            s2[pl.ds(start + 2 * jj, 32, stride=8), :] = first[own]
            s2[pl.ds(start + 2 * jj + 1, 32, stride=8), :] = second[own]
        send_all(farthest_first([dz]), s2, r2, 8, 8, f_send, f_recv.at[my_z])
    keep_own(s2, r2, 8, 8)
    send_all(everyone, ms, mr, 8, 1, m_send, m_recv)
    keep_own(ms, mr, 8, 1)

    t = 2.0 + (lam_ref[...] + eig)
    u2 = t * t - 1.0
    u3 = t * (t * t - 2.0)
    w3 = 1.0 / u3
    w1 = u2 * w3
    w2 = t * w3
    f1, f2, f3 = (spec[:, r * NZ : (r + 1) * NZ] for r in range(1, ROWS))
    modal[:, 0:NZ] = w1 * f1 + w2 * f2 + w3 * f3
    modal[:, NZ : 2 * NZ] = w2 * (f1 + t * f2 + f3)
    modal[:, 2 * NZ : 3 * NZ] = w3 * f1 + w2 * f2 + w1 * f3
    wrow[:, 0:NZ] = w1
    wrow[:, NZ : 2 * NZ] = w2
    wrow[:, 2 * NZ : 3 * NZ] = w3

    for jj in range(4):
        shift = lam_ref[pl.ds(my_z * 128 + jj * 32 + (me - my_z * 32), 1), :] + eig
        edge = 2.0 + shift
        inv[:, jj * NZ : (jj + 1) * NZ] = 1.0 / (
            edge * edge * shift * (4.0 + shift) + lamx_ref[...]
        )
    for copy in large[6:]:
        copy.wait()
    spectral = None
    for group, dz in enumerate((2, 3, 1, 0)):
        z = z_of[dz]
        wait_rows(r2, (32 if dz else 31) * 8, f_recv.at[z])
        for jj in range(4):
            for h in range(2):
                first = pl.multiple_of(z * 256, 256) + 2 * jj + h
                high, low = split(r2[pl.ds(first, 32, stride=8), :])
                for part, value in enumerate((high, low, high)):
                    start = group * 192 + part * 64 + h * 32
                    xk[start : start + 32, jj * NZ : (jj + 1) * NZ] = value
        piece = mm(hxf_ref[z], xk[group * 192 : (group + 1) * 192, :])
        spectral = piece if spectral is None else spectral + piece
    solved = spectral * inv[...]
    high, low = split(solved)
    xk[0:RANKS, :] = high
    xk[RANKS : 2 * RANKS, :] = low
    xk[2 * RANKS : 3 * RANKS, :] = high
    for dz in (2, 1, 3, 0):
        z = z_of[dz]
        for h in range(2):
            face = mm(
                hxi_ref[pl.ds(pl.multiple_of(h * RANKS + z * 32, 32), 32), :], xk[0 : 3 * RANKS, :]
            )
            for jj in range(4):
                first = pl.multiple_of(z * 256, 256) + 2 * jj + h
                s3[pl.ds(first, 32, stride=8), :] = face[:, jj * NZ : (jj + 1) * NZ]
        send_all(farthest_first([dz]), s3, r3, 8, 8, b_send, b_recv.at[my_z])
    keep_own(s3, r3, 8, 8)

    wait_rows(mr, RANKS - 1, m_recv)
    thinning = lax.dot_general(
        pick, mr[pl.ds(0, RANKS, stride=8), :], contract_first,
        precision=lax.Precision.HIGHEST, preferred_element_type=F32,
    )
    thick_ref[...] = ice_ref[...] - 0.3 * thinning

    for group, dz in enumerate((2, 3, 1, 0)):
        z = z_of[dz]
        wait_rows(r3, (32 if dz else 31) * 8, b_recv.at[z])
        for jj in range(4):
            first = pl.multiple_of(z * 256, 256) + 2 * jj
            q0 = r3[pl.ds(first, 32, stride=8), :]
            q1 = r3[pl.ds(first + 1, 32, stride=8), :]
            rows = pl.ds(pl.multiple_of(z * BLK, BLK) + jj * 32, 32)
            w1, w2, w3 = (wrow[rows, r * NZ : (r + 1) * NZ] for r in range(3))
            fields = [
                q0,
                w1 * q0 + w3 * q1 + modal[rows, 0:NZ],
                w2 * (q0 + q1) + modal[rows, NZ : 2 * NZ],
                w3 * q0 + w1 * q1 + modal[rows, 2 * NZ : 3 * NZ],
            ]
            for r in range(ROWS):
                high, low = split(fields[r])
                for part, value in enumerate((high, low, high)):
                    start = group * 3 * BLK + part * BLK + jj * 32
                    x3[start : start + 32, r * NZ : (r + 1) * NZ] = value
        right = x3[group * 3 * BLK : (group + 1) * 3 * BLK, 0 : ROWS * NZ]
        if group == 0:
            acc[...] = mm(hb[z], right)
        else:
            acc[...] += mm(hb[z], right)

    wait_rows(xs, RANKS - 1, c_send)
    wait_rows(s2, (RANKS - 1) * 8, f_send)
    wait_rows(ms, RANKS - 1, m_send)
    wait_rows(s3, (RANKS - 1) * 8, b_send)


def synthesis_kernel(back, thickness, synth, out_hbm, thick_hbm, pressure, sem):
    thick = pltpu.make_async_copy(thickness, thick_hbm, sem.at[NB])
    thick.start()
    synth_high, synth_low = split(synth[...])
    synth_both = jnp.concatenate([synth_high, synth_low], axis=1)
    stores = []
    for i in range(NB):
        rows = pl.ds(i * BLK, BLK)
        for r in range(ROWS):
            high, low = split(back[rows, r * NZ : (r + 1) * NZ])
            wide = mm(high, synth_both)
            pressure[r, rows, :] = wide[:, 0:NZ] + wide[:, NZ:] + mm(low, synth_high)
        stores.append(
            pltpu.make_async_copy(pressure.at[:, rows], out_hbm.at[:, rows], sem.at[i])
        )
        stores[-1].start()
    for copy in stores + [thick]:
        copy.wait()


def body(
    velocity,
    layer_depth,
    vertical_modes,
    vertical_synthesis,
    mode_eigen,
    boundary_tracers,
    friction_speed,
    draft_level,
    tile_offset,
    draft_count,
    draft_list,
    exchange_coeff,
    ice_thickness,
):
    hh, hl = split_table(hartley(NY))
    small = hartley(RANKS)
    following = (np.arange(RANKS) + 1) % RANKS
    fwd_high, fwd_low = split_table(np.concatenate([small, small[:, following]], axis=1))
    inv_high, inv_low = split_table(np.concatenate([small, small[following]], axis=0))
    hxf = np.stack(
        [
            np.concatenate(
                [
                    table[:, half * RANKS + z * 32 : half * RANKS + (z + 1) * 32]
                    for table in (fwd_high, fwd_high, fwd_low)
                    for half in range(2)
                ],
                axis=1,
            )
            for z in range(4)
        ]
    )
    hxi = np.concatenate([inv_high, inv_high, inv_low], axis=1)
    lam = np.repeat(eigen(NY)[:, None], NZ, axis=1).astype(np.float32)
    lamx = np.repeat(eigen(RANKS)[:, None], NZ, axis=1).astype(np.float32)
    vmem = pl.BlockSpec(memory_space=pltpu.VMEM)
    hbm = pl.BlockSpec(memory_space=pltpu.HBM)
    tiles = (RANKS * 8, NZ)
    results = pl.pallas_call(
        kernel,
        out_shape=(
            jax.ShapeDtypeStruct((NY, ROWS * NZ), F32),
            jax.ShapeDtypeStruct((16, 128), F32),
        ),
        in_specs=[hbm] * 18,
        out_specs=(vmem, vmem),
        scratch_shapes=[
            pltpu.VMEM((4, RANKS, 192), BF16),
            pltpu.VMEM((2 * RANKS, 3 * RANKS), BF16),
            pltpu.VMEM((NY, NZ), F32),
            pltpu.VMEM((RANKS, NZ), F32),
            pltpu.VMEM((1, NZ), F32),
            pltpu.VMEM((NZ, NZ), F32),
            pltpu.VMEM((16, 128), F32),
            pltpu.VMEM((1, NZ), F32),
            pltpu.VMEM((2, ROWS, NY), F32),
            pltpu.VMEM((ROWS, NY), F32),
            pltpu.VMEM((ROWS, NY), jnp.int32),
            pltpu.VMEM((1, RANKS), jnp.int32),
            pltpu.VMEM((1, RANKS), jnp.int32),
            pltpu.VMEM((8, RANKS), jnp.int32),
            pltpu.VMEM((16, 128), F32),
            pltpu.VMEM((3, ROWS, NY, NZ), F32),
            pltpu.VMEM((NY, 3 * NY), BF16),
            pltpu.VMEM((3 * NY, (ROWS + 1) * NZ), BF16),
            pltpu.VMEM((NY, ROWS * NZ), F32),
            pltpu.VMEM((NY, (ROWS + 1) * NZ), F32),
            pltpu.VMEM((NY, ROWS * NZ), F32),
            pltpu.VMEM((6 * RANKS, 4 * NZ), BF16),
            pltpu.VMEM((RANKS, 4 * NZ), F32),
            pltpu.VMEM(tiles, F32),
            pltpu.VMEM(tiles, F32),
            pltpu.VMEM(tiles, F32),
            pltpu.VMEM(tiles, F32),
            pltpu.VMEM(tiles, F32),
            pltpu.VMEM(tiles, F32),
            pltpu.VMEM(tiles, F32),
            pltpu.VMEM(tiles, F32),
            pltpu.VMEM((NB, NY, 3 * BLK), BF16),
            pltpu.SemaphoreType.DMA((31,)),
            pltpu.SemaphoreType.DMA,
            pltpu.SemaphoreType.DMA,
            pltpu.SemaphoreType.DMA,
            pltpu.SemaphoreType.DMA,
            pltpu.SemaphoreType.DMA,
            pltpu.SemaphoreType.DMA((4,)),
            pltpu.SemaphoreType.DMA,
            pltpu.SemaphoreType.DMA((4,)),
        ],
        compiler_params=pltpu.CompilerParams(
            collective_id=0, has_side_effects=True, vmem_limit_bytes=32 * 2**20
        ),
    )(*(pltpu.with_memory_space_constraint(jnp.asarray(x), pltpu.HBM) for x in (
        velocity,
        hh,
        hl,
        hxf,
        hxi,
        lam,
        lamx,
        layer_depth.reshape(1, NZ),
        vertical_modes,
        ice_thickness.reshape(16, 128),
        mode_eigen.reshape(1, NZ),
        boundary_tracers,
        friction_speed,
        draft_level,
        tile_offset.reshape(1, RANKS),
        draft_count,
        jnp.swapaxes(draft_list, 1, 2).reshape(8, RANKS),
        exchange_coeff.reshape(16, 128),
    )))
    pressure, thickness = pl.pallas_call(
        synthesis_kernel,
        out_shape=(
            jax.ShapeDtypeStruct((ROWS, NY, NZ), F32),
            jax.ShapeDtypeStruct((16, 128), F32),
        ),
        in_specs=[vmem] * 3,
        out_specs=(hbm, hbm),
        scratch_shapes=[
            pltpu.VMEM((ROWS, NY, NZ), F32),
            pltpu.SemaphoreType.DMA((NB + 1,)),
        ],
        compiler_params=pltpu.CompilerParams(vmem_limit_bytes=16 * 2**20),
    )(*results, vertical_synthesis)
    return (pressure, thickness.reshape(2048))


def solution(mesh):
    in_specs = (
        P(None, ("px", "py"), None, None),
        P(),
        P(),
        P(),
        P(),
        P(None, ("px", "py"), None),
        P(("px", "py"), None),
        P(("px", "py"), None),
        P(),
        P(("px", "py"), None),
        P(("px", "py"), None, None),
        P(("px", "py")),
        P(("px", "py")),
    )
    out_specs = (P(("px", "py"), None, None), P(("px", "py")))
    return jax.shard_map(body, mesh=mesh, in_specs=in_specs, out_specs=out_specs, check_vma=False)
```

```python
import math
import random

import jax
import jax.numpy as jnp
import numpy as np
from jax import lax
from jax.experimental import pallas as pl
from jax.experimental.pallas import tpu as pltpu
from jax.sharding import PartitionSpec as P

NX = 512
NY = 512
NZ = 128
RANKS = 128
ROWS = 4
NB = 4
BLK = NY // NB
MESH = pl.DeviceIdType.MESH
F32 = jnp.float32
BF16 = jnp.bfloat16


def hops(offset):
    dz, dy, dx, dc = offset
    return sum(min(d, 4 - d) for d in (dz, dy, dx))


def farthest_first(dzs):
    offsets = [
        (dz, dy, dx, dc)
        for dz in dzs
        for dy in range(4)
        for dx in range(4)
        for dc in range(2)
        if (dz, dy, dx, dc) != (0, 0, 0, 0)
    ]
    random.Random(2).shuffle(offsets)
    return sorted(offsets, key=lambda offset: -hops(offset))


def hartley(length):
    index = np.arange(length)
    angle = (np.outer(index, index) % length) * (2.0 * math.pi / length)
    return (np.cos(angle) + np.sin(angle)) / math.sqrt(length)


def split_table(table):
    high = np.asarray(table, np.float32).astype(jnp.bfloat16)
    low = (np.asarray(table, np.float32) - high.astype(np.float32)).astype(jnp.bfloat16)
    return high, low


def eigen(length):
    return 2.0 - 2.0 * np.cos(2.0 * math.pi * np.arange(length) / length)


def split(x):
    high = x.astype(BF16)
    return high, (x - high.astype(F32)).astype(BF16)


def mm(a, b):
    return jnp.dot(a, b, preferred_element_type=F32)


def mm_exact_left(a, x):
    high, low = split(x)
    return mm(a, high) + mm(a, low)


def mm_exact_right(x, b):
    high, low = split(x)
    return mm(high, b) + mm(low, b)


def mm3(x, b_high, b_low):
    high, low = split(x)
    return mm(high, b_high) + mm(low, b_high) + mm(high, b_low)


def iota(shape, axis):
    return lax.broadcasted_iota(jnp.int32, shape, axis)


def kernel(
    vel_hbm,
    hh_hbm,
    hl_hbm,
    hxf_hbm,
    hxi_hbm,
    lam_hbm,
    lamx_hbm,
    depth_hbm,
    modes_hbm,
    ice_hbm,
    eig_hbm,
    trac_hbm,
    fric_hbm,
    lvl_hbm,
    off_hbm,
    cnt_hbm,
    list_hbm,
    coeff_hbm,
    acc,
    thick_ref,
    hxf_ref,
    hxi_ref,
    lam_ref,
    lamx_ref,
    depth_ref,
    modes_ref,
    ice_ref,
    eig_ref,
    trac_ref,
    fric_ref,
    lvl_ref,
    off_ref,
    cnt_ref,
    list_ref,
    coeff_ref,
    vel,
    h3,
    x3,
    modal,
    spec,
    wrow,
    xk,
    inv,
    xs,
    xr,
    ms,
    mr,
    s2,
    r2,
    s3,
    r3,
    hb,
    load_sem,
    c_send,
    c_recv,
    m_send,
    m_recv,
    f_send,
    f_recv,
    b_send,
    b_recv,
):
    px = lax.axis_index("px")
    py = lax.axis_index("py")
    my_z, my_c, my_y, my_x = px // 2, px % 2, py // 4, py % 4
    me = px * 16 + py

    def load(source, target, index):
        return pltpu.make_async_copy(source, target, load_sem.at[index])

    small = [
        load(source, target, index)
        for index, (source, target) in enumerate(
            (
                (off_hbm, off_ref),
                (coeff_hbm, coeff_ref),
                (trac_hbm, trac_ref),
                (fric_hbm, fric_ref),
                (lvl_hbm, lvl_ref),
                (cnt_hbm, cnt_ref),
                (list_hbm, list_ref),
                (depth_hbm, depth_ref),
                (modes_hbm, modes_ref),
                (eig_hbm, eig_ref),
            )
        )
    ]
    large = [
        load(source, target, index + len(small))
        for index, (source, target) in enumerate(
            (
                (vel_hbm, vel),
                (hh_hbm, h3.at[:, pl.ds(0, NY)]),
                (hh_hbm, h3.at[:, pl.ds(NY, NY)]),
                (hl_hbm, h3.at[:, pl.ds(2 * NY, NY)]),
                (lam_hbm, lam_ref),
                (lamx_hbm, lamx_ref),
                (hxf_hbm, hxf_ref),
                (hxi_hbm, hxi_ref),
                (ice_hbm, ice_ref),
            )
            + tuple(
                (
                    table.at[:, pl.ds(b * BLK, BLK)],
                    hb.at[b, :, pl.ds(part * BLK, BLK)],
                )
                for b in range(NB)
                for part, table in enumerate((hh_hbm, hh_hbm, hl_hbm))
            )
        )
    ]

    z_of = [(my_z + d) % 4 for d in range(4)]
    c_of = [my_c, 1 - my_c]
    px_of = [[z_of[dz] * 2 + c_of[dc] for dc in range(2)] for dz in range(4)]
    py_of = [[(my_y + dy) % 4 * 4 + (my_x + dx) % 4 for dx in range(4)] for dy in range(4)]
    everyone = farthest_first(range(4))
    barrier = pltpu.get_barrier_semaphore()
    for dz, dy, dx, dc in everyone:
        pl.semaphore_signal(
            barrier, inc=1, device_id=(px_of[dz][dc], py_of[dy][dx]), device_id_type=MESH
        )

    for copy in small + large:
        copy.start()
    for copy in small:
        copy.wait()

    off = off_ref[...]
    sub = iota((RANKS, RANKS), 0)
    lane = iota((RANKS, RANKS), 1)
    tile_row = (iota((RANKS, 16), 0) // 8 == iota((RANKS, 16), 1)).astype(BF16)
    pick = mm(((me - off + RANKS) % RANKS == sub).astype(BF16), tile_row)
    xs[pl.ds(0, RANKS, stride=8), :] = jnp.dot(
        pick, coeff_ref[...], precision=lax.Precision.HIGHEST
    )

    def send_all(offsets, source, target, unit, rows, send_sem, recv_sem):
        for dz, dy, dx, dc in offsets:
            dest_px, dest_py = px_of[dz][dc], py_of[dy][dx]
            first = pl.multiple_of((dest_px * 16 + dest_py) * unit, unit)
            pltpu.make_async_remote_copy(
                src_ref=source.at[pl.ds(first, rows), :],
                dst_ref=target.at[pl.ds(pl.multiple_of(me * unit, unit), rows), :],
                send_sem=send_sem,
                recv_sem=recv_sem,
                device_id=(dest_px, dest_py),
                device_id_type=MESH,
            ).start()

    def keep_own(source, target, unit, rows):
        own = pl.ds(pl.multiple_of(me * unit, unit), rows)
        target[own, :] = source[own, :]

    def wait_rows(ref, rows, sem):
        pltpu.make_async_copy(ref.at[pl.ds(0, rows), :], ref.at[pl.ds(0, rows), :], sem).wait()

    pl.semaphore_wait(barrier, RANKS - 1)
    send_all(everyone, xs, xr, 8, 1, c_send, c_recv)
    keep_own(xs, xr, 8, 1)

    inv_depth = 1.0 / depth_ref[...]
    inv_depth_col = jnp.sum(jnp.where(sub == lane, inv_depth, 0.0), axis=1, keepdims=True)
    level = lvl_ref[...].astype(F32)
    thermal = trac_ref[0] - 0.6 * trac_ref[1] + 1.5 * ((level + 0.5) / NZ) - 0.5
    factor = fric_ref[...] * thermal
    rows_lane = (iota((ROWS, NZ), 1) % 16 // 4 == iota((ROWS, NZ), 0)).astype(F32)
    contract_first = (((0,), (0,)), ((), ()))
    factor_lanes = lax.dot_general(
        factor, rows_lane, contract_first, precision=lax.Precision.HIGHEST,
        preferred_element_type=F32,
    )
    y_sub = iota((NY, NZ), 0)
    y_lane = iota((NY, NZ), 1)
    in_tile = y_sub % 32 == 4 * (y_lane // 16) + y_lane % 4
    tile_of_y = (iota((NY, RANKS), 0) // 4 == iota((NY, RANKS), 1)).astype(BF16)
    tile_from_y = (iota((RANKS, NY), 1) // 4 == iota((RANKS, NY), 0)).astype(BF16)
    by_tile = mm_exact_left(tile_from_y, jnp.where(in_tile, factor_lanes, 0.0))
    cells = jnp.where(iota((8, RANKS), 0) < cnt_ref[...], list_ref[...], -1).astype(F32)
    slot_spread = (iota((8, 8 * NZ), 1) // NZ == iota((8, 8 * NZ), 0)).astype(F32)
    cell_lanes = lax.dot_general(
        cells, slot_spread, contract_first, preferred_element_type=F32
    )
    position = (lane % 16).astype(F32)
    live = cell_lanes[:, 0:NZ] == position
    for slot in range(1, 8):
        live = jnp.logical_or(live, cell_lanes[:, slot * NZ : (slot + 1) * NZ] == position)
    to_owner = ((me + off) % RANKS == sub).astype(BF16)
    factor_owner = mm_exact_left(to_owner, jnp.where(live, by_tile, 0.0))
    owner_of_y = lax.dot_general(
        tile_of_y, to_owner, (((1,), (1,)), ((), ())), preferred_element_type=F32
    ).astype(BF16)

    modes = modes_ref[...]
    mode_high, mode_low = split(modes)
    scaled_high, scaled_low = split(modes * inv_depth_col)
    spread = (iota((ROWS, ROWS * NZ), 1) // NZ == iota((ROWS, ROWS * NZ), 0)).astype(F32)
    level_lanes = lax.dot_general(
        level, spread, contract_first, preferred_element_type=F32
    )
    for r in range(ROWS):
        hot = (level_lanes[:, r * NZ : (r + 1) * NZ] == y_lane.astype(F32)).astype(BF16)
        wrow[:, r * NZ : (r + 1) * NZ] = mm(hot, scaled_high) + mm(hot, scaled_low)
    large[0].wait()

    def put_split(field, r):
        high, low = split(field)
        x3[0:NY, r * NZ : (r + 1) * NZ] = high
        x3[NY : 2 * NY, r * NZ : (r + 1) * NZ] = low
        x3[2 * NY : 3 * NY, r * NZ : (r + 1) * NZ] = high

    def divergence(r):
        east, north, up = vel[0, r], vel[1, r], vel[2, r]
        if r > 0:
            east = east - vel[0, r - 1]
        below = jnp.where(y_lane == 0, 0.0, pltpu.roll(up, 1, axis=1))
        flow = east + (north - pltpu.roll(north, 1, axis=0)) + (up - below) * inv_depth
        modal[:, r * NZ : (r + 1) * NZ] = mm3(flow, mode_high, mode_low)

    for r in range(ROWS):
        divergence(r)
    put_split(mm3(vel[0, ROWS - 1], mode_high, mode_low), ROWS)
    for copy in large[1:6]:
        copy.wait()
    spec[:, ROWS * NZ : (ROWS + 1) * NZ] = mm(h3[...], x3[:, ROWS * NZ : (ROWS + 1) * NZ])
    spread_rows = (
        iota((NZ, ROWS * NZ), 0) % 16 // 4 == iota((NZ, ROWS * NZ), 1) // NZ
    ).astype(BF16)

    wait_rows(xr, RANKS - 1, c_recv)
    melt = xr[pl.ds(0, RANKS, stride=8), :] * factor_owner
    ms[pl.ds(0, RANKS, stride=8), :] = melt
    by_y = jnp.where(in_tile, mm_exact_left(owner_of_y, melt), 0.0)
    melt_lanes = mm_exact_right(by_y, spread_rows)
    for r in range(ROWS):
        cols = slice(r * NZ, (r + 1) * NZ)
        put_split(modal[:, cols] + melt_lanes[:, cols] * wrow[:, cols], r)

    eig = eig_ref[...]

    for dz in (2, 1, 3, 0):
        rows = pl.ds(pl.multiple_of(z_of[dz] * BLK, BLK), BLK)
        part = mm(h3[rows, :], x3[:, 0 : ROWS * NZ])
        spec[rows, 0 : ROWS * NZ] = part
        t = 2.0 + (lam_ref[rows, :] + eig)
        u2 = t * t - 1.0
        u3 = t * (t * t - 2.0)
        f = [part[:, r * NZ : (r + 1) * NZ] for r in range(ROWS)]
        first = u3 * f[0] + u2 * f[1] + t * f[2] + f[3]
        second = f[1] + t * f[2] + u2 * f[3] - u3 * spec[rows, ROWS * NZ : (ROWS + 1) * NZ]
        start = pl.multiple_of(z_of[dz] * 256, 256)
        for jj in range(4):
            own = slice(jj * 32, (jj + 1) * 32)
            s2[pl.ds(start + 2 * jj, 32, stride=8), :] = first[own]
            s2[pl.ds(start + 2 * jj + 1, 32, stride=8), :] = second[own]
        send_all(farthest_first([dz]), s2, r2, 8, 8, f_send, f_recv.at[my_z])
    keep_own(s2, r2, 8, 8)
    send_all(everyone, ms, mr, 8, 1, m_send, m_recv)
    keep_own(ms, mr, 8, 1)

    t = 2.0 + (lam_ref[...] + eig)
    u2 = t * t - 1.0
    u3 = t * (t * t - 2.0)
    w3 = 1.0 / u3
    w1 = u2 * w3
    w2 = t * w3
    f1, f2, f3 = (spec[:, r * NZ : (r + 1) * NZ] for r in range(1, ROWS))
    modal[:, 0:NZ] = w1 * f1 + w2 * f2 + w3 * f3
    modal[:, NZ : 2 * NZ] = w2 * (f1 + t * f2 + f3)
    modal[:, 2 * NZ : 3 * NZ] = w3 * f1 + w2 * f2 + w1 * f3
    wrow[:, 0:NZ] = w1
    wrow[:, NZ : 2 * NZ] = w2
    wrow[:, 2 * NZ : 3 * NZ] = w3

    for jj in range(4):
        shift = lam_ref[pl.ds(my_z * 128 + jj * 32 + (me - my_z * 32), 1), :] + eig
        edge = 2.0 + shift
        inv[:, jj * NZ : (jj + 1) * NZ] = 1.0 / (
            edge * edge * shift * (4.0 + shift) + lamx_ref[...]
        )
    for copy in large[6:]:
        copy.wait()
    spectral = None
    for group, dz in enumerate((2, 3, 1, 0)):
        z = z_of[dz]
        wait_rows(r2, (32 if dz else 31) * 8, f_recv.at[z])
        for jj in range(4):
            for h in range(2):
                first = pl.multiple_of(z * 256, 256) + 2 * jj + h
                high, low = split(r2[pl.ds(first, 32, stride=8), :])
                for part, value in enumerate((high, low, high)):
                    start = group * 192 + part * 64 + h * 32
                    xk[start : start + 32, jj * NZ : (jj + 1) * NZ] = value
        piece = mm(hxf_ref[z], xk[group * 192 : (group + 1) * 192, :])
        spectral = piece if spectral is None else spectral + piece
    solved = spectral * inv[...]
    high, low = split(solved)
    xk[0:RANKS, :] = high
    xk[RANKS : 2 * RANKS, :] = low
    xk[2 * RANKS : 3 * RANKS, :] = high
    for dz in (2, 1, 3, 0):
        z = z_of[dz]
        for h in range(2):
            face = mm(
                hxi_ref[pl.ds(pl.multiple_of(h * RANKS + z * 32, 32), 32), :], xk[0 : 3 * RANKS, :]
            )
            for jj in range(4):
                first = pl.multiple_of(z * 256, 256) + 2 * jj + h
                s3[pl.ds(first, 32, stride=8), :] = face[:, jj * NZ : (jj + 1) * NZ]
        send_all(farthest_first([dz]), s3, r3, 8, 8, b_send, b_recv.at[my_z])
    keep_own(s3, r3, 8, 8)

    wait_rows(mr, RANKS - 1, m_recv)
    thinning = lax.dot_general(
        pick, mr[pl.ds(0, RANKS, stride=8), :], contract_first,
        precision=lax.Precision.HIGHEST, preferred_element_type=F32,
    )
    thick_ref[...] = ice_ref[...] - 0.3 * thinning

    for group, dz in enumerate((2, 3, 1, 0)):
        z = z_of[dz]
        wait_rows(r3, (32 if dz else 31) * 8, b_recv.at[z])
        for jj in range(4):
            first = pl.multiple_of(z * 256, 256) + 2 * jj
            q0 = r3[pl.ds(first, 32, stride=8), :]
            q1 = r3[pl.ds(first + 1, 32, stride=8), :]
            rows = pl.ds(pl.multiple_of(z * BLK, BLK) + jj * 32, 32)
            w1, w2, w3 = (wrow[rows, r * NZ : (r + 1) * NZ] for r in range(3))
            fields = [
                q0,
                w1 * q0 + w3 * q1 + modal[rows, 0:NZ],
                w2 * (q0 + q1) + modal[rows, NZ : 2 * NZ],
                w3 * q0 + w1 * q1 + modal[rows, 2 * NZ : 3 * NZ],
            ]
            for r in range(ROWS):
                high, low = split(fields[r])
                for part, value in enumerate((high, low, high)):
                    start = group * 3 * BLK + part * BLK + jj * 32
                    x3[start : start + 32, r * NZ : (r + 1) * NZ] = value
        right = x3[group * 3 * BLK : (group + 1) * 3 * BLK, 0 : ROWS * NZ]
        if group == 0:
            acc[...] = mm(hb[z], right)
        else:
            acc[...] += mm(hb[z], right)

    wait_rows(xs, RANKS - 1, c_send)
    wait_rows(s2, (RANKS - 1) * 8, f_send)
    wait_rows(ms, RANKS - 1, m_send)
    wait_rows(s3, (RANKS - 1) * 8, b_send)


def synthesis_kernel(back, thickness, synth, out_hbm, thick_hbm, pressure, sem):
    thick = pltpu.make_async_copy(thickness, thick_hbm, sem.at[NB])
    thick.start()
    synth_high, synth_low = split(synth[...])
    synth_both = jnp.concatenate([synth_high, synth_low], axis=1)
    stores = []
    for i in range(NB):
        rows = pl.ds(i * BLK, BLK)
        for r in range(ROWS):
            high, low = split(back[rows, r * NZ : (r + 1) * NZ])
            wide = mm(high, synth_both)
            pressure[r, rows, :] = wide[:, 0:NZ] + wide[:, NZ:] + mm(low, synth_high)
        stores.append(
            pltpu.make_async_copy(pressure.at[:, rows], out_hbm.at[:, rows], sem.at[i])
        )
        stores[-1].start()
    for copy in stores + [thick]:
        copy.wait()


def body(
    velocity,
    layer_depth,
    vertical_modes,
    vertical_synthesis,
    mode_eigen,
    boundary_tracers,
    friction_speed,
    draft_level,
    tile_offset,
    draft_count,
    draft_list,
    exchange_coeff,
    ice_thickness,
):
    hh, hl = split_table(hartley(NY))
    small = hartley(RANKS)
    following = (np.arange(RANKS) + 1) % RANKS
    fwd_high, fwd_low = split_table(np.concatenate([small, small[:, following]], axis=1))
    inv_high, inv_low = split_table(np.concatenate([small, small[following]], axis=0))
    hxf = np.stack(
        [
            np.concatenate(
                [
                    table[:, half * RANKS + z * 32 : half * RANKS + (z + 1) * 32]
                    for table in (fwd_high, fwd_high, fwd_low)
                    for half in range(2)
                ],
                axis=1,
            )
            for z in range(4)
        ]
    )
    hxi = np.concatenate([inv_high, inv_high, inv_low], axis=1)
    lam = np.repeat(eigen(NY)[:, None], NZ, axis=1).astype(np.float32)
    lamx = np.repeat(eigen(RANKS)[:, None], NZ, axis=1).astype(np.float32)
    vmem = pl.BlockSpec(memory_space=pltpu.VMEM)
    hbm = pl.BlockSpec(memory_space=pltpu.HBM)
    tiles = (RANKS * 8 + 8, NZ)
    results = pl.pallas_call(
        kernel,
        out_shape=(
            jax.ShapeDtypeStruct((NY, ROWS * NZ), F32),
            jax.ShapeDtypeStruct((16, 128), F32),
        ),
        in_specs=[hbm] * 18,
        out_specs=(vmem, vmem),
        scratch_shapes=[
            pltpu.VMEM((4, RANKS, 192), BF16),
            pltpu.VMEM((2 * RANKS, 3 * RANKS), BF16),
            pltpu.VMEM((NY, NZ), F32),
            pltpu.VMEM((RANKS, NZ), F32),
            pltpu.VMEM((1, NZ), F32),
            pltpu.VMEM((NZ, NZ), F32),
            pltpu.VMEM((16, 128), F32),
            pltpu.VMEM((1, NZ), F32),
            pltpu.VMEM((2, ROWS, NY), F32),
            pltpu.VMEM((ROWS, NY), F32),
            pltpu.VMEM((ROWS, NY), jnp.int32),
            pltpu.VMEM((1, RANKS), jnp.int32),
            pltpu.VMEM((1, RANKS), jnp.int32),
            pltpu.VMEM((8, RANKS), jnp.int32),
            pltpu.VMEM((16, 128), F32),
            pltpu.VMEM((3, ROWS, NY, NZ), F32),
            pltpu.VMEM((NY, 3 * NY), BF16),
            pltpu.VMEM((3 * NY, (ROWS + 1) * NZ), BF16),
            pltpu.VMEM((NY, ROWS * NZ), F32),
            pltpu.VMEM((NY, (ROWS + 1) * NZ), F32),
            pltpu.VMEM((NY, ROWS * NZ), F32),
            pltpu.VMEM((6 * RANKS, 4 * NZ), BF16),
            pltpu.VMEM((RANKS, 4 * NZ), F32),
            pltpu.VMEM(tiles, F32),
            pltpu.VMEM(tiles, F32),
            pltpu.VMEM(tiles, F32),
            pltpu.VMEM(tiles, F32),
            pltpu.VMEM(tiles, F32),
            pltpu.VMEM(tiles, F32),
            pltpu.VMEM(tiles, F32),
            pltpu.VMEM(tiles, F32),
            pltpu.VMEM((NB, NY, 3 * BLK), BF16),
            pltpu.SemaphoreType.DMA((31,)),
            pltpu.SemaphoreType.DMA,
            pltpu.SemaphoreType.DMA,
            pltpu.SemaphoreType.DMA,
            pltpu.SemaphoreType.DMA,
            pltpu.SemaphoreType.DMA,
            pltpu.SemaphoreType.DMA((4,)),
            pltpu.SemaphoreType.DMA,
            pltpu.SemaphoreType.DMA((4,)),
        ],
        compiler_params=pltpu.CompilerParams(
            collective_id=0, has_side_effects=True, vmem_limit_bytes=32 * 2**20
        ),
    )(*(pltpu.with_memory_space_constraint(jnp.asarray(x), pltpu.HBM) for x in (
        velocity,
        hh,
        hl,
        hxf,
        hxi,
        lam,
        lamx,
        layer_depth.reshape(1, NZ),
        vertical_modes,
        ice_thickness.reshape(16, 128),
        mode_eigen.reshape(1, NZ),
        boundary_tracers,
        friction_speed,
        draft_level,
        tile_offset.reshape(1, RANKS),
        draft_count,
        jnp.swapaxes(draft_list, 1, 2).reshape(8, RANKS),
        exchange_coeff.reshape(16, 128),
    )))
    pressure, thickness = pl.pallas_call(
        synthesis_kernel,
        out_shape=(
            jax.ShapeDtypeStruct((ROWS, NY, NZ), F32),
            jax.ShapeDtypeStruct((16, 128), F32),
        ),
        in_specs=[vmem] * 3,
        out_specs=(hbm, hbm),
        scratch_shapes=[
            pltpu.VMEM((ROWS, NY, NZ), F32),
            pltpu.SemaphoreType.DMA((NB + 1,)),
        ],
        compiler_params=pltpu.CompilerParams(vmem_limit_bytes=16 * 2**20),
    )(*results, vertical_synthesis)
    return (pressure, thickness.reshape(2048))


def solution(mesh):
    in_specs = (
        P(None, ("px", "py"), None, None),
        P(),
        P(),
        P(),
        P(),
        P(None, ("px", "py"), None),
        P(("px", "py"), None),
        P(("px", "py"), None),
        P(),
        P(("px", "py"), None),
        P(("px", "py"), None, None),
        P(("px", "py")),
        P(("px", "py")),
    )
    out_specs = (P(("px", "py"), None, None), P(("px", "py")))
    return jax.shard_map(body, mesh=mesh, in_specs=in_specs, out_specs=out_specs, check_vma=False)
```
